128 devices in a mesh: ia: 16 (over z, x_lo, core), ka: 8 (over y, x_hi).
Axes of the slice: x: 4 (x_hi: 2, x_lo: 2; x = x_hi * 2 + x_lo), y: 4, z: 4, core: 2. Of those that a mesh axis runs over, the one named last changes fastest.
Arguments:
- amplitudes: float32 [16, 16, 1024, 1024], P('ia', 'ka'), may hold values from -3 to 3
- integrals: bfloat16 [16, 2, 16, 1024, 1024], P('ia', None, 'ka'), may hold values from -0.046875 to 0.046875
- tile_mask: int32 [16, 2, 16, 8, 8], P('ia', None, 'ka'), may hold values from 0 to 1, as said below
- pair_list: int32 [16, 2], replicated, may hold values from 0 to 15, as said below
Outputs:
- residual: float32 [16, 2, 1024, 1024], P('ia', None, 'ka')
The draws below stay inside these ranges and needn't reach their ends.
Inputs may be any that keep to these rules, and one draw needn't show every extreme that they name: `tile_mask`: 1 marks a filled 128 x 128 tile of an integral block, 0 an empty one. `pair_list`: row i names two different occupied indices, neither equal to i; j stands in row i exactly when i stands in row j.
All inputs are finite; a program needn't handle non-finite values.
Results may differ from the reference program's by a relative error of at most 0.0003.
Values sent between devices are 32-bit elements; how exact they have to be, the bound alone decides.
A program may use at most 192 MiB of HBM per device.

```python
import jax
import jax.numpy as jnp
from jax import lax

V = 1024
VT = 128
NT = 8
NO = 16


def draw_tile_mask(key, part):
    level_key = jax.random.fold_in(key, 11)
    tile_key = jax.random.fold_in(key, 23)
    level = jax.random.randint(level_key, (NO, 2, NO, 1, 1), 4, 9)
    tiles = jax.random.randint(tile_key, (NO, 2, NO, NT, NT), 0, 8)
    return (tiles < level).astype(jnp.int32)


def draw_pair_list(key, part):
    order = jax.random.permutation(jax.random.fold_in(key, 5), NO).astype(jnp.int32)
    before = jnp.roll(order, 1)
    after = jnp.roll(order, -1)
    pairs = jnp.stack([before, after], axis=1)
    return jnp.zeros((NO, 2), jnp.int32).at[order].set(pairs)


def steps_of(stream_key, extent, shards, low, largest):
    loudness, own = 1.0, jax.random.fold_in(stream_key, 6)
    for dim, blocks in shards:
        draws = jnp.exp(jax.random.uniform(jax.random.fold_in(own, dim), (blocks,), jnp.float32, low / len(shards), largest / len(shards)))
        loudness = loudness * jnp.repeat(draws, extent[dim] // blocks).reshape([-1 if axis == dim else 1 for axis in range(len(extent))])
    return loudness


def gaussian(rng, shape, width, most, split=(), kind=jnp.bfloat16):
    values = width * jax.random.normal(rng, shape, jnp.float32)
    if split:
        values = values * steps_of(rng, shape, split, -0.22, 0.18)
    return jnp.clip(values, -most, most).astype(kind)


def setup_inputs(seed: int = 0) -> dict:
    keys = jax.random.split(jax.random.key(seed), 5)
    return {
        "amplitudes": gaussian(keys[0], (NO, NO, V, V), 0.5, 3.0, ((0, 16), (1, 8)), jnp.float32),
        "integrals": gaussian(keys[1], (NO, 2, NO, V, V), (NO * V) ** -0.5, 0.046875, ((0, 16), (2, 8))),
        "tile_mask": draw_tile_mask(jax.random.fold_in(keys[4], 71), 0),
        "pair_list": draw_pair_list(jax.random.fold_in(keys[4], 71), 0),
    }


def expand_mask(tile_mask, tile_side):
    grown = jnp.repeat(jnp.repeat(tile_mask, tile_side, axis=-2), tile_side, axis=-1)
    return grown.astype(jnp.float32)


def reference(amplitudes, integrals, tile_mask, pair_list):
    def one_row(index):
        mixed = 2.0 * amplitudes[index] - jnp.swapaxes(amplitudes[:, index], 1, 2)
        masked = integrals[index].astype(jnp.float32) * expand_mask(tile_mask[index], VT)
        return jnp.einsum("kxy,skyz->sxz", mixed, masked, precision=lax.Precision.HIGHEST)

    partial_value = lax.map(one_row, jnp.arange(NO, dtype=jnp.int32))
    owners = jnp.arange(NO, dtype=jnp.int32)
    partner_slot = jnp.where(pair_list[pair_list, 0] == owners[:, None], 0, 1).astype(jnp.int32)
    return partial_value + jnp.swapaxes(partial_value[pair_list, partner_slot], 2, 3)
```

```python
import jax
import jax.numpy as jnp
from jax import lax
from jax.experimental import pallas as pl
from jax.experimental.pallas import tpu as pltpu
from jax.sharding import PartitionSpec as P

MESH = pl.DeviceIdType.MESH
HBM = pl.BlockSpec(memory_space=pl.ANY)

SIDE = 4
STEPS = ((1, 0, 0), (-1, 0, 0), (0, 1, 0), (0, -1, 0), (0, 0, 1), (0, 0, -1))
HOPS = 16
LAG = 2
SUBS = 2 * HOPS
CROSS_OWN = 3


def position():
    ia, ka = lax.axis_index("ia"), lax.axis_index("ka")
    return (ka % 2) * 2 + (ia // 2) % 2, ka // 2, ia // 4, ia % 2


def device(x, y, z, core):
    return z * 4 + (x % 2) * 2 + core, y * 2 + x // 2


def pick(test, then, other):
    return jnp.where(test, then, other)


def own_slot(index):
    return pick(index < CROSS_OWN, index, 2 * index - 2)


def relay_slot(index):
    return pick(index > 5, index + 8, 2 * index + 3)


def landing(x, y, z, half, index):
    apart = (z - y + SIDE) % SIDE
    inner = (x == 1) | (x == 2)
    x_way = pick(half == 0, 2 - x, x - 1)
    even = index % 2 == 0
    two_way = pick(half == 0, pick(even, 4, 5), pick(even, 2, 3))
    way = pick(
        apart == 0,
        pick(inner, x_way, 6 + half),
        pick(apart == 1, pick(half == 0, 4, 3), pick(apart == 3, pick(half == 0, 5, 2), two_way)),
    )
    slot = pick(apart == 2, relay_slot(index // 2), index)
    return way, slot


def mirror_kernel(t_ref, land, arrive, leave, swap_arrive, swap_leave):
    x, y, z, core = position()
    inner = (x == 1) | (x == 2)
    apart = (z - y + SIDE) % SIDE
    alone = (apart == 0) & jnp.logical_not(inner)

    def towards(way):
        dx, dy, dz = STEPS[way]
        return (x + dx + SIDE) % SIDE, (y + dy + SIDE) % SIDE, (z + dz + SIDE) % SIDE

    barrier = pltpu.get_barrier_semaphore()
    for way in range(6):
        for other in range(2):
            pl.semaphore_signal(barrier, inc=1, device_id=device(*towards(way), other), device_id_type=MESH)
    pl.semaphore_signal(barrier, inc=1, device_id=device(x, y, z, 1 - core), device_id_type=MESH)
    pl.semaphore_wait(barrier, 13)

    def swap(half):
        return pltpu.make_async_remote_copy(
            src_ref=t_ref.at[1 - core, pl.ds(half * HOPS, HOPS)],
            dst_ref=land.at[6 + half, :, core],
            send_sem=swap_leave.at[half],
            recv_sem=swap_arrive.at[half],
            device_id=device(x, y, z, 1 - core),
            device_id_type=MESH,
        )

    @pl.when(alone)
    def _():
        swap(0).start()
        swap(1).start()

    def landed(way, slot):
        pltpu.make_async_copy(land.at[way, slot], land.at[way, slot], arrive.at[way, slot]).wait()

    def send_own(way, slot, sub):
        for block in range(2):
            pltpu.make_async_remote_copy(
                src_ref=t_ref.at[block, sub],
                dst_ref=land.at[way, slot, core],
                send_sem=leave.at[way, slot],
                recv_sem=arrive.at[way, slot],
                device_id=device(*towards(way), block),
                device_id_type=MESH,
            ).start()

    def send_on(way, slot, from_way, from_slot):
        pltpu.make_async_remote_copy(
            src_ref=land.at[from_way, from_slot],
            dst_ref=land.at[way, slot],
            send_sem=leave.at[way, slot],
            recv_sem=arrive.at[way, slot],
            device_id=device(*towards(way), core),
            device_id_type=MESH,
        ).start()

    near_y = pick(inner, LAG, 0)
    near_z = pick(inner, 3 * LAG, 0)
    far_y = pick(inner, 4, 0)
    far_z = pick(inner, 4 + 2 * LAG, 0)

    relay_from = {2: (5, -1, 4, 4), 3: (4, 5, 5, -1), 4: (3, 2, 2, -1), 5: (2, -1, 3, 3)}

    def by_apart(values):
        zero, one, two, three = values
        return pick(apart == 0, zero, pick(apart == 1, one, pick(apart == 2, two, three)))

    def yz_lag(way):
        along_y = way < 4
        own, cross = (near_y, far_y) if along_y else (near_z, far_z)
        through = near_z if along_y else near_y
        passing = far_z if along_y else far_y
        values = [through + LAG, passing + LAG, cross, passing + LAG]
        for place, source in enumerate(relay_from[way]):
            if source < 0:
                values[place] = own
        return by_apart(values)

    lags = [
        pick(inner, 0, pick(x == 3, LAG, 2 * LAG)),
        pick(inner, 0, pick(x == 0, LAG, 2 * LAG)),
    ] + [yz_lag(way) for way in range(2, 6)]

    def step(t, carry):
        for way in range(6):
            slot = t - lags[way]
            active = (slot >= 0) & (slot < HOPS)
            if way < 2:
                half = pick(x == 1 + way, 0, 1)
                from_t, sub = inner, half * HOPS + slot
                from_way, from_slot = way, slot
            else:
                half = 0 if way < 4 else 1
                odd = way % 2
                early, late = slot < CROSS_OWN, slot > 13
                relayed = late | (jnp.logical_not(early) & (slot % 2 == 1))
                own_index = pick(early, slot, (slot + 2) // 2)
                relay_index = pick(late, slot - 8, (slot - 3) // 2)
                index = pick(apart == 2, 2 * own_index + odd, slot)
                places = relay_from[way]
                near_own = by_apart([places[0] < 0, places[1] < 0, False, places[3] < 0])
                own = pick(apart == 2, jnp.logical_not(relayed), near_own)
                from_t = own & jnp.logical_not(inner)
                sub = half * HOPS + index
                x_way = (2 - x) if half == 0 else (x - 1)
                relay_way = by_apart([max(place, 0) for place in places])
                from_way = pick(own, x_way, relay_way)
                from_slot = pick(own, index, pick(apart == 2, own_slot(relay_index), slot))

            @pl.when(active & from_t)
            def _(way=way, slot=slot, sub=sub):
                send_own(way, slot, sub)

            @pl.when(active & jnp.logical_not(from_t))
            def _(way=way, slot=slot, from_way=from_way, from_slot=from_slot):
                landed(from_way, from_slot)
                send_on(way, slot, from_way, from_slot)

        return carry

    lax.fori_loop(0, HOPS + 4 + 3 * LAG, step, 0)

    @pl.when(jnp.logical_not(alone))
    def _():
        def finish(index, carry):
            for half in range(2):
                landed(*landing(x, y, z, half, index))
            return carry

        lax.fori_loop(0, HOPS, finish, 0)

    @pl.when(alone)
    def _():
        swap(0).wait()
        swap(1).wait()

    def drain(slot, carry):
        for way in range(6):
            pltpu.make_async_copy(land.at[way, slot], land.at[way, slot], leave.at[way, slot]).wait()
        return carry

    lax.fori_loop(0, HOPS, drain, 0)


def mirror(amplitudes):
    blocks, virtuals = amplitudes.shape[0], amplitudes.shape[2]
    rows = virtuals // SUBS
    return pl.pallas_call(
        mirror_kernel,
        out_shape=jax.ShapeDtypeStruct((8, HOPS, blocks, rows, virtuals), jnp.float32),
        in_specs=[HBM],
        out_specs=HBM,
        scratch_shapes=[
            pltpu.SemaphoreType.DMA((6, HOPS)),
            pltpu.SemaphoreType.DMA((6, HOPS)),
            pltpu.SemaphoreType.DMA((2,)),
            pltpu.SemaphoreType.DMA((2,)),
        ],
        compiler_params=pltpu.CompilerParams(collective_id=0, has_side_effects=True),
    )(amplitudes.reshape(blocks, SUBS, rows, virtuals))


ROW_BLOCK = 256


def product_kernel(t_ref, land, w_ref, mask_ref, out_ref, t_buf, m_buf, w_buf, o_buf, t_sem, m_sem, w_sem, o_sem):
    x, y, z, core = position()
    alone = (z == y) & jnp.logical_not((x == 1) | (x == 2))
    blocks, virtuals = t_ref.shape[0], t_ref.shape[2]
    rows = virtuals // SUBS
    slots = w_ref.shape[0]
    tiles = 8
    tile = virtuals // tiles

    for block in range(blocks):
        pltpu.make_async_copy(t_ref.at[block], t_buf.at[block], t_sem.at[block]).start()

        @pl.when(alone & (core == block))
        def _(block=block):
            pltpu.make_async_copy(t_ref.at[block], m_buf.at[block], m_sem.at[block]).start()

        @pl.when(jnp.logical_not(alone & (core == block)))
        def _(block=block):
            def fetch(index, carry):
                for half in range(2):
                    way, slot = landing(x, y, z, half, index)
                    first = (half * HOPS + index) * rows
                    pltpu.make_async_copy(
                        land.at[way, slot, block],
                        m_buf.at[block, pl.ds(pl.multiple_of(first, rows), rows)],
                        m_sem.at[block],
                    ).start()
                return carry

            lax.fori_loop(0, HOPS, fetch, 0)

        for s in range(slots):
            pltpu.make_async_copy(w_ref.at[s, block], w_buf.at[s, block], w_sem.at[s, block]).start()

    for block in range(blocks):
        for s in range(slots):
            pltpu.make_async_copy(w_ref.at[s, block], w_buf.at[s, block], w_sem.at[s, block]).wait()

            def scale(r, carry, s=s, block=block):
                band = pl.ds(pl.multiple_of(r * tile, tile), tile)
                for c in range(tiles):
                    keep = mask_ref[((s * blocks + block) * tiles + r) * tiles + c]
                    columns = pl.ds(c * tile, tile)
                    value = w_buf[s, block, band, columns]
                    w_buf[s, block, band, columns] = jnp.where(keep != 0, value, jnp.zeros_like(value))
                return carry

            lax.fori_loop(0, tiles, scale, 0)

    for block in range(blocks):
        pltpu.make_async_copy(t_ref.at[block], t_buf.at[block], t_sem.at[block]).wait()
        pltpu.make_async_copy(t_ref.at[block], m_buf.at[block], m_sem.at[block]).wait()

    def band_of(b, carry):
        band = pl.ds(pl.multiple_of(b * ROW_BLOCK, ROW_BLOCK), ROW_BLOCK)
        halves = []
        for block in range(blocks):
            mixed = 2.0 * t_buf[block, band, :] - m_buf[block, :, band].T
            high = mixed.astype(jnp.bfloat16)
            low = (mixed - high.astype(jnp.float32)).astype(jnp.bfloat16)
            halves.append(jnp.concatenate([high, low], axis=0))
        for s in range(slots):
            total = jnp.zeros((2 * ROW_BLOCK, virtuals), jnp.float32)
            for block in range(blocks):
                total += jnp.dot(halves[block], w_buf[s, block], preferred_element_type=jnp.float32)
            o_buf[s, band, :] = total[:ROW_BLOCK] + total[ROW_BLOCK:]
            pltpu.make_async_copy(o_buf.at[s, band], out_ref.at[s, band], o_sem.at[s, b]).start()
        return carry

    bands = virtuals // ROW_BLOCK
    lax.fori_loop(0, bands, band_of, 0)
    for b in range(bands):
        for s in range(slots):
            band = pl.ds(b * ROW_BLOCK, ROW_BLOCK)
            pltpu.make_async_copy(o_buf.at[s, band], out_ref.at[s, band], o_sem.at[s, b]).wait()


def product(amplitudes, land, integrals, tile_mask):
    slots, blocks, virtuals = integrals.shape[0], integrals.shape[1], integrals.shape[2]
    return pl.pallas_call(
        product_kernel,
        out_shape=jax.ShapeDtypeStruct((slots, virtuals, virtuals), jnp.float32),
        in_specs=[HBM, HBM, HBM, pl.BlockSpec(memory_space=pltpu.SMEM)],
        out_specs=HBM,
        scratch_shapes=[
            pltpu.VMEM((blocks, virtuals, virtuals), jnp.float32),
            pltpu.VMEM((blocks, virtuals, virtuals), jnp.float32),
            pltpu.VMEM((slots, blocks, virtuals, virtuals), jnp.bfloat16),
            pltpu.VMEM((slots, virtuals, virtuals), jnp.float32),
            pltpu.SemaphoreType.DMA((blocks,)),
            pltpu.SemaphoreType.DMA((blocks,)),
            pltpu.SemaphoreType.DMA((slots, blocks)),
            pltpu.SemaphoreType.DMA((slots, virtuals // ROW_BLOCK)),
        ],
        compiler_params=pltpu.CompilerParams(vmem_limit_bytes=58 << 20),
    )(amplitudes, land, integrals, tile_mask.reshape(-1))


def body(amplitudes, integrals, tile_mask, pair_list):
    land = mirror(amplitudes[0])
    partial_value = product(amplitudes[0], land, integrals[0], tile_mask[0])
    own_rows = lax.psum_scatter(partial_value, "ka", scatter_dimension=1, tiled=True)
    columns = lax.all_to_all(own_rows, "ka", split_axis=2, concat_axis=1, tiled=True)
    flipped = jnp.swapaxes(columns, 1, 2)
    spread = lax.all_to_all(flipped, "ia", split_axis=1, concat_axis=0, tiled=True)
    occupied = pair_list.shape[0]
    owners = jnp.arange(occupied, dtype=jnp.int32)
    partner_slot = jnp.where(pair_list[pair_list, 0] == owners[:, None], 0, 1).astype(jnp.int32)
    source_row = pair_list * 2 + partner_slot
    routed = jnp.take(spread, source_row.reshape(-1), axis=0)
    routed = routed.reshape(occupied, 2, spread.shape[1], spread.shape[2])
    delivered = lax.all_to_all(routed, "ia", split_axis=0, concat_axis=2, tiled=True)
    return (own_rows + delivered[0])[None]


def solution(mesh):
    placed = (
        P("ia", "ka", None, None),
        P("ia", None, "ka", None, None),
        P("ia", None, "ka", None, None),
        P(),
    )
    return jax.shard_map(
        body, mesh=mesh, in_specs=placed, out_specs=P("ia", None, "ka", None), check_vma=False
    )
```

```python
import jax
import jax.numpy as jnp
from jax import lax
from jax.experimental import pallas as pl
from jax.experimental.pallas import tpu as pltpu
from jax.sharding import PartitionSpec as P

MESH = pl.DeviceIdType.MESH
HBM = pl.BlockSpec(memory_space=pl.ANY)

SIDE = 4
STEPS = ((1, 0, 0), (-1, 0, 0), (0, 1, 0), (0, -1, 0), (0, 0, 1), (0, 0, -1))
HOPS = 32
LAG = 2
SUBS = 2 * HOPS
CROSS_OWN = 3
BAND = 256
CHUNKS = 4


def position():
    ia, ka = lax.axis_index("ia"), lax.axis_index("ka")
    return (ka % 2) * 2 + (ia // 2) % 2, ka // 2, ia // 4, ia % 2


def towards(x, y, z, way):
    dx, dy, dz = STEPS[way]
    return (x + dx + SIDE) % SIDE, (y + dy + SIDE) % SIDE, (z + dz + SIDE) % SIDE


def device(x, y, z, core):
    return z * 4 + (x % 2) * 2 + core, y * 2 + x // 2


def pick(test, then, other):
    return jnp.where(test, then, other)


def own_slot(index):
    return pick(index < CROSS_OWN, index, 2 * index - 2)


def relay_slot(index):
    return pick(index > HOPS // 2 - 3, index + HOPS // 2, 2 * index + 3)


def landing(x, y, z, half, index):
    apart = (z - y + SIDE) % SIDE
    x_way = pick(half == 0, 2 - x, x - 1)
    even = index % 2 == 0
    two_way = pick(half == 0, pick(even, 4, 5), pick(even, 2, 3))
    way = pick(
        apart == 0,
        x_way,
        pick(apart == 1, pick(half == 0, 4, 3), pick(apart == 3, pick(half == 0, 5, 2), two_way)),
    )
    slot = pick(apart == 2, relay_slot(index // 2), index)
    return way, slot


def exchange(t_ref, land, m_buf, arrive, leave, m_sem, swap_arrive, swap_leave):
    x, y, z, core = position()
    inner = (x == 1) | (x == 2)
    apart = (z - y + SIDE) % SIDE
    alone = (apart == 0) & jnp.logical_not(inner)

    def swap(half):
        return pltpu.make_async_remote_copy(
            src_ref=t_ref.at[1 - core, pl.ds(half * HOPS, HOPS)],
            dst_ref=m_buf.at[core, pl.ds(half * HOPS, HOPS)],
            send_sem=swap_leave.at[half],
            recv_sem=swap_arrive.at[half],
            device_id=device(x, y, z, 1 - core),
            device_id_type=MESH,
        )

    @pl.when(alone)
    def _():
        swap(0).start()
        swap(1).start()
        pltpu.make_async_copy(t_ref.at[core], m_buf.at[core], m_sem).start()

    def landed(way, slot):
        pltpu.make_async_copy(land.at[way, slot], land.at[way, slot], arrive.at[way, slot]).wait()

    def send_own(way, slot, sub):
        for block in range(2):
            pltpu.make_async_remote_copy(
                src_ref=t_ref.at[block, sub],
                dst_ref=land.at[way, slot, core],
                send_sem=leave.at[way, slot],
                recv_sem=arrive.at[way, slot],
                device_id=device(*towards(x, y, z, way), block),
                device_id_type=MESH,
            ).start()

    def send_on(way, slot, from_way, from_slot):
        pltpu.make_async_remote_copy(
            src_ref=land.at[from_way, from_slot],
            dst_ref=land.at[way, slot],
            send_sem=leave.at[way, slot],
            recv_sem=arrive.at[way, slot],
            device_id=device(*towards(x, y, z, way), core),
            device_id_type=MESH,
        ).start()

    near_y = pick(inner, LAG, 0)
    near_z = pick(inner, 3 * LAG, 0)
    far_y = pick(inner, 4, 0)
    far_z = pick(inner, 4 + 2 * LAG, 0)

    relay_from = {2: (5, -1, 4, 4), 3: (4, 5, 5, -1), 4: (3, 2, 2, -1), 5: (2, -1, 3, 3)}

    def by_apart(values):
        zero, one, two, three = values
        return pick(apart == 0, zero, pick(apart == 1, one, pick(apart == 2, two, three)))

    def yz_lag(way):
        along_y = way < 4
        own, cross = (near_y, far_y) if along_y else (near_z, far_z)
        through = near_z if along_y else near_y
        passing = far_z if along_y else far_y
        values = [through + LAG, passing + LAG, cross, passing + LAG]
        for place, source in enumerate(relay_from[way]):
            if source < 0:
                values[place] = own
        return by_apart(values)

    lags = [
        pick(inner, 0, pick(x == 3, LAG, 2 * LAG)),
        pick(inner, 0, pick(x == 0, LAG, 2 * LAG)),
    ] + [yz_lag(way) for way in range(2, 6)]

    def step(t, carry):
        for way in range(6):
            slot = t - lags[way]
            active = (slot >= 0) & (slot < HOPS)
            if way < 2:
                half = pick(x == 1 + way, 0, 1)
                from_t, sub = inner, half * HOPS + slot
                from_way, from_slot = way, slot
            else:
                half = 0 if way < 4 else 1
                odd = way % 2
                early, late = slot < CROSS_OWN, slot > HOPS - 3
                relayed = late | (jnp.logical_not(early) & (slot % 2 == 1))
                own_index = pick(early, slot, (slot + 2) // 2)
                relay_index = pick(late, slot - HOPS // 2, (slot - 3) // 2)
                index = pick(apart == 2, 2 * own_index + odd, slot)
                places = relay_from[way]
                near_own = by_apart([places[0] < 0, places[1] < 0, False, places[3] < 0])
                own = pick(apart == 2, jnp.logical_not(relayed), near_own)
                from_t = own & jnp.logical_not(inner)
                sub = half * HOPS + index
                x_way = (2 - x) if half == 0 else (x - 1)
                relay_way = by_apart([max(place, 0) for place in places])
                from_way = pick(own, x_way, relay_way)
                from_slot = pick(own, index, pick(apart == 2, own_slot(relay_index), slot))

            @pl.when(active & from_t)
            def _(way=way, slot=slot, sub=sub):
                send_own(way, slot, sub)

            @pl.when(active & jnp.logical_not(from_t))
            def _(way=way, slot=slot, from_way=from_way, from_slot=from_slot):
                landed(from_way, from_slot)
                send_on(way, slot, from_way, from_slot)

        return carry

    lax.fori_loop(0, HOPS + 4 + 3 * LAG, step, 0)

    @pl.when(jnp.logical_not(alone))
    def _():
        def finish(index, carry):
            for half in range(2):
                way, slot = landing(x, y, z, half, index)
                landed(way, slot)
                pltpu.make_async_copy(land.at[way, slot], m_buf.at[:, half * HOPS + index], m_sem).start()
            return carry

        lax.fori_loop(0, HOPS, finish, 0)
        pltpu.make_async_copy(m_buf, m_buf, m_sem).wait()

    @pl.when(alone)
    def _():
        swap(0).wait()
        swap(1).wait()
        pltpu.make_async_copy(t_ref.at[core], m_buf.at[core], m_sem).wait()


def drain_exchange(land, leave):
    def drain(slot, carry):
        for way in range(6):
            pltpu.make_async_copy(land.at[way, slot], land.at[way, slot], leave.at[way, slot]).wait()
        return carry

    lax.fori_loop(0, HOPS, drain, 0)


def cycle_kernel(
    t_ref, w_ref, mask_ref, land, out_ref,
    t_buf, m_buf, w_buf, o_buf, ring, relay, inbox,
    arrive, leave, t_sem, m_sem, w_sem, swap_arrive, swap_leave,
    ring_arrive, ring_leave, relay_arrive, relay_leave, inbox_arrive, inbox_leave,
):
    x, y, z, core = position()
    slots, blocks, virtuals = w_buf.shape[0], w_buf.shape[1], w_buf.shape[2]

    barrier = pltpu.get_barrier_semaphore()
    for way in range(6):
        for other in range(2):
            pl.semaphore_signal(
                barrier, inc=1, device_id=device(*towards(x, y, z, way), other), device_id_type=MESH
            )
    pl.semaphore_signal(barrier, inc=1, device_id=device(x, y, z, 1 - core), device_id_type=MESH)
    pl.semaphore_wait(barrier, 13)

    load_t = pltpu.make_async_copy(t_ref, t_buf, t_sem)
    load_w = pltpu.make_async_copy(w_ref, w_buf, w_sem)
    load_t.start()
    load_w.start()

    exchange(t_ref, land, m_buf, arrive, leave, m_sem, swap_arrive, swap_leave)

    load_t.wait()
    load_w.wait()
    tiles = 8
    tile = virtuals // tiles

    def mask_band(n, carry):
        s, block, r = n // (blocks * tiles), (n // tiles) % blocks, n % tiles
        band = pl.ds(pl.multiple_of(r * tile, tile), tile)
        for c in range(tiles):
            keep = mask_ref[n * tiles + c]
            columns = pl.ds(c * tile, tile)
            value = w_buf[s, block, band, columns]
            w_buf[s, block, band, columns] = jnp.where(keep != 0, value, jnp.zeros_like(value))
        return carry

    lax.fori_loop(0, slots * blocks * tiles, mask_band, 0)

    x_half = x // 2
    part = BAND // CHUNKS

    def band_of(s, k):
        return pick(s == 0, y + SIDE - 1 - k, y + 1 + k) % SIDE

    def rows_of(band, chunk):
        offset = pick(chunk < 2, (1 - x_half) * (BAND // 2), x_half * (BAND // 2) - BAND // 2) + chunk * part
        return pl.ds(pl.multiple_of(band * BAND + offset, part), part)

    def ring_copy(s, k, chunk):
        return pltpu.make_async_remote_copy(
            src_ref=o_buf.at[s, rows_of(band_of(s, k), chunk)],
            dst_ref=ring.at[s, k, chunk],
            send_sem=ring_leave.at[s, k, chunk],
            recv_sem=ring_arrive.at[s, k, chunk],
            device_id=device(x, (y + pick(s == 0, 1, SIDE - 1)) % SIDE, z, core),
            device_id_type=MESH,
        )

    def x_beside(s):
        return device((x + pick(s == 0, 1, SIDE - 1)) % SIDE, y, z, core)

    def relay_copy(s, chunk):
        return pltpu.make_async_remote_copy(
            src_ref=o_buf.at[s, rows_of(y, chunk)],
            dst_ref=relay.at[s, chunk],
            send_sem=relay_leave.at[s, chunk],
            recv_sem=relay_arrive.at[s, chunk],
            device_id=x_beside(s),
            device_id_type=MESH,
        )

    def inbox_copy(s, chunk):
        return pltpu.make_async_remote_copy(
            src_ref=relay.at[s, chunk],
            dst_ref=inbox.at[s, chunk],
            send_sem=inbox_leave.at[s, chunk],
            recv_sem=inbox_arrive.at[s, chunk],
            device_id=x_beside(s),
            device_id_type=MESH,
        )

    def absorb(s, k, chunk):
        ring_copy(s, k - 1, chunk).wait_recv()
        rows = rows_of(band_of(s, k), chunk)
        o_buf[s, rows, :] = o_buf[s, rows, :] + ring[s, k - 1, chunk]

    def unit(u, carry):
        s = u % 2
        band = pl.ds(pl.multiple_of(band_of(s, u // 2) * BAND, BAND), BAND)
        total = jnp.zeros((2 * BAND, virtuals), jnp.float32)
        for block in range(blocks):
            mirrored = m_buf[block, :, :, band].reshape(virtuals, BAND).T
            mixed = 2.0 * t_rows(block, u) - mirrored
            high = mixed.astype(jnp.bfloat16)
            low = (mixed - high.astype(jnp.float32)).astype(jnp.bfloat16)
            pair = jnp.concatenate([high, low], axis=0)
            total += jnp.dot(pair, w_buf[s, block], preferred_element_type=jnp.float32)
        o_buf[s, band, :] = total[:BAND] + total[BAND:]

        @pl.when(u < 2)
        def _():
            for chunk in range(CHUNKS):
                ring_copy(s, 0, chunk).start()

        @pl.when((u >= 3) & (u < 3 + CHUNKS))
        def _():
            for way in range(2):
                absorb(way, 1, u - 3)
                ring_copy(way, 1, u - 3).start()

        return carry

    def t_rows(block, u):
        band = band_of(u % 2, u // 2)
        subs = BAND // t_buf.shape[2]
        return t_buf[block, pl.ds(band * subs, subs)].reshape(BAND, virtuals)

    lax.fori_loop(0, slots * SIDE, unit, 0)

    def second(chunk, carry):
        for s in range(2):
            absorb(s, 2, chunk)
            ring_copy(s, 2, chunk).start()
        return carry

    lax.fori_loop(0, CHUNKS, second, 0)

    def third(chunk, carry):
        for s in range(2):
            absorb(s, 3, chunk)

        @pl.when(chunk < 2)
        def _():
            for s in range(2):
                relay_copy(s, chunk).start()

        @pl.when(chunk >= 2)
        def _():
            for s in range(2):
                relay_copy(s, chunk - 2).wait_recv()
                inbox_copy(s, chunk - 2).start()

        return carry

    lax.fori_loop(0, CHUNKS, third, 0)

    for chunk in range(2):
        for s in range(2):
            inbox_copy(s, chunk).wait_recv()
            out_ref[s, pl.ds(chunk * part, part), :] = o_buf[s, rows_of(y, chunk + 2), :] + inbox[s, chunk]

    def drain(chunk, carry):
        for s in range(2):
            for k in range(3):
                ring_copy(s, k, chunk).wait_send()
        return carry

    lax.fori_loop(0, CHUNKS, drain, 0)
    for chunk in range(2):
        for s in range(2):
            relay_copy(s, chunk).wait_send()
            inbox_copy(s, chunk).wait_send()
    drain_exchange(land, leave)


def summed_rows(amplitudes, integrals, tile_mask):
    slots, blocks, virtuals = integrals.shape[0], integrals.shape[1], integrals.shape[2]
    rows = virtuals // SUBS
    part = BAND // CHUNKS
    dma = pltpu.SemaphoreType.DMA
    return pl.pallas_call(
        cycle_kernel,
        out_shape=(
            jax.ShapeDtypeStruct((6, HOPS, blocks, rows, virtuals), jnp.float32),
            jax.ShapeDtypeStruct((slots, BAND // 2, virtuals), jnp.float32),
        ),
        in_specs=[HBM, HBM, pl.BlockSpec(memory_space=pltpu.SMEM)],
        out_specs=(HBM, pl.BlockSpec(memory_space=pltpu.VMEM)),
        scratch_shapes=[
            pltpu.VMEM((blocks, SUBS, rows, virtuals), jnp.float32),
            pltpu.VMEM((blocks, SUBS, rows, virtuals), jnp.float32),
            pltpu.VMEM((slots, blocks, virtuals, virtuals), jnp.bfloat16),
            pltpu.VMEM((slots, virtuals, virtuals), jnp.float32),
            pltpu.VMEM((slots, 3, CHUNKS, part, virtuals), jnp.float32),
            pltpu.VMEM((slots, 2, part, virtuals), jnp.float32),
            pltpu.VMEM((slots, 2, part, virtuals), jnp.float32),
            dma((6, HOPS)),
            dma((6, HOPS)),
            dma,
            dma,
            dma,
            dma((2,)),
            dma((2,)),
            dma((slots, 3, CHUNKS)),
            dma((slots, 3, CHUNKS)),
            dma((slots, 2)),
            dma((slots, 2)),
            dma((slots, 2)),
            dma((slots, 2)),
        ],
        compiler_params=pltpu.CompilerParams(
            collective_id=0, has_side_effects=True, vmem_limit_bytes=58 << 20
        ),
    )(amplitudes.reshape(blocks, SUBS, rows, virtuals), integrals, tile_mask.reshape(-1))[1]


def body(amplitudes, integrals, tile_mask, pair_list):
    own_rows = summed_rows(amplitudes[0], integrals[0], tile_mask[0])
    row_groups, col_groups = lax.axis_size("ia"), lax.axis_size("ka")
    slots, rows, virtuals = own_rows.shape
    thin, wide = rows // row_groups, virtuals // col_groups
    pieces = own_rows.reshape(slots, row_groups, thin, col_groups, wide).transpose(1, 3, 0, 2, 4)
    pieces = pieces.reshape(row_groups * col_groups, slots, thin, wide)
    spread = lax.all_to_all(pieces, ("ia", "ka"), split_axis=0, concat_axis=0, tiled=True)
    spread = spread.reshape(row_groups, col_groups, slots, thin, wide).transpose(0, 2, 1, 3, 4)
    spread = spread.reshape(row_groups * slots, col_groups, thin, wide)
    owners = jnp.arange(row_groups, dtype=jnp.int32)
    partner_slot = jnp.where(pair_list[pair_list, 0] == owners[:, None], 0, 1).astype(jnp.int32)
    source_row = pair_list * 2 + partner_slot
    routed = jnp.take(spread, source_row.reshape(-1), axis=0)
    routed = routed.reshape(row_groups, slots, col_groups, thin, wide)
    delivered = lax.all_to_all(routed, "ia", split_axis=0, concat_axis=0, tiled=True)
    mirrored = delivered.transpose(1, 4, 2, 0, 3).reshape(slots, wide, virtuals)
    return (own_rows + mirrored)[None]


def solution(mesh):
    placed = (
        P("ia", "ka", None, None),
        P("ia", None, "ka", None, None),
        P("ia", None, "ka", None, None),
        P(),
    )
    return jax.shard_map(
        body, mesh=mesh, in_specs=placed, out_specs=P("ia", None, "ka", None), check_vma=False
    )
```

```python
import jax
import jax.numpy as jnp
from jax import lax
from jax.experimental import pallas as pl
from jax.experimental.pallas import tpu as pltpu
from jax.sharding import PartitionSpec as P

MESH = pl.DeviceIdType.MESH
HBM = pl.BlockSpec(memory_space=pl.ANY)

SIDE = 4
STEPS = ((1, 0, 0), (-1, 0, 0), (0, 1, 0), (0, -1, 0), (0, 0, 1), (0, 0, -1))
HOPS = 32
LAG = 2
LATE = HOPS // 2
SUBS = 2 * HOPS
CROSS_OWN = 3
BAND = 256


def position():
    ia, ka = lax.axis_index("ia"), lax.axis_index("ka")
    return (ka % 2) * 2 + (ia // 2) % 2, ka // 2, ia // 4, ia % 2


def towards(x, y, z, way):
    dx, dy, dz = STEPS[way]
    return (x + dx + SIDE) % SIDE, (y + dy + SIDE) % SIDE, (z + dz + SIDE) % SIDE


def device(x, y, z, core):
    return z * 4 + (x % 2) * 2 + core, y * 2 + x // 2


def pick(test, then, other):
    return jnp.where(test, then, other)


def own_slot(index):
    return pick(index < CROSS_OWN, index, 2 * index - 2)


def relay_slot(index):
    return pick(index > HOPS // 2 - 3, index + HOPS // 2, 2 * index + 3)


def yz_rest(y, z, half, index):
    apart = (z - y + SIDE) % SIDE
    even = index % 2 == 0
    two_way = pick(half == 0, pick(even, 4, 5), pick(even, 2, 3))
    way = pick(apart == 1, pick(half == 0, 4, 3), pick(apart == 3, pick(half == 0, 5, 2), two_way))
    return way, pick(apart == 2, relay_slot(index // 2), index)


def x_rest(x, half, index):
    return pick(half == 0, 2 - x, x - 1), (index + LATE) % HOPS


def landing(x, y, z, half, index):
    inner = (x == 1) | (x == 2)
    by_x = inner & ((index < LATE) | (y == z))
    way, slot = yz_rest(y, z, half, index)
    x_way, x_slot = x_rest(x, half, index)
    return pick(by_x, x_way, way), pick(by_x, x_slot, slot)


def exchange(t_ref, land, m_buf, arrive, leave, m_sem, swap_arrive, swap_leave):
    x, y, z, core = position()
    inner = (x == 1) | (x == 2)
    apart = (z - y + SIDE) % SIDE
    alone = (apart == 0) & jnp.logical_not(inner)

    def swap(half):
        return pltpu.make_async_remote_copy(
            src_ref=t_ref.at[1 - core, pl.ds(half * HOPS, HOPS)],
            dst_ref=m_buf.at[core, pl.ds(half * HOPS, HOPS)],
            send_sem=swap_leave.at[half],
            recv_sem=swap_arrive.at[half],
            device_id=device(x, y, z, 1 - core),
            device_id_type=MESH,
        )

    @pl.when(alone)
    def _():
        swap(0).start()
        swap(1).start()
        pltpu.make_async_copy(t_ref.at[core], m_buf.at[core], m_sem).start()

    def landed(way, slot):
        pltpu.make_async_copy(land.at[way, slot], land.at[way, slot], arrive.at[way, slot]).wait()

    def send_own(way, slot, sub):
        for block in range(2):
            pltpu.make_async_remote_copy(
                src_ref=t_ref.at[block, sub],
                dst_ref=land.at[way, slot, core],
                send_sem=leave.at[way, slot],
                recv_sem=arrive.at[way, slot],
                device_id=device(*towards(x, y, z, way), block),
                device_id_type=MESH,
            ).start()

    def send_on(way, slot, from_way, from_slot):
        pltpu.make_async_remote_copy(
            src_ref=land.at[from_way, from_slot],
            dst_ref=land.at[way, slot],
            send_sem=leave.at[way, slot],
            recv_sem=arrive.at[way, slot],
            device_id=device(*towards(x, y, z, way), core),
            device_id_type=MESH,
        ).start()

    relay_from = {2: (5, -1, 4, 4), 3: (4, 5, 5, -1), 4: (3, 2, 2, -1), 5: (2, -1, 3, 3)}

    def by_apart(values):
        zero, one, two, three = values
        return pick(apart == 0, zero, pick(apart == 1, one, pick(apart == 2, two, three)))

    def yz_lag(way):
        return by_apart([0 if source < 0 or place == 2 else LAG for place, source in enumerate(relay_from[way])])

    lags = [
        pick(inner, 0, pick(x == 3, LAG, 2 * LAG)),
        pick(inner, 0, pick(x == 0, LAG, 2 * LAG)),
    ] + [yz_lag(way) for way in range(2, 6)]

    def step(t, carry):
        for way in range(6):
            slot = t - lags[way]
            active = (slot >= 0) & (slot < HOPS)
            if way < 2:
                half = pick(x == 1 + way, 0, 1)
                index = (slot + LATE) % HOPS
                from_t = inner & ((slot < LATE) | (apart == 0))
                sub = half * HOPS + index
                rest_way, rest_slot = yz_rest(y, z, half, index)
                from_way, from_slot = pick(inner, rest_way, way), pick(inner, rest_slot, slot)
            else:
                half = 0 if way < 4 else 1
                odd = way % 2
                early, late = slot < CROSS_OWN, slot > HOPS - 3
                relayed = late | (jnp.logical_not(early) & (slot % 2 == 1))
                own_index = pick(early, slot, (slot + 2) // 2)
                relay_index = pick(late, slot - HOPS // 2, (slot - 3) // 2)
                index = pick(apart == 2, 2 * own_index + odd, slot)
                places = relay_from[way]
                near_own = by_apart([places[0] < 0, places[1] < 0, False, places[3] < 0])
                own = pick(apart == 2, jnp.logical_not(relayed), near_own)
                from_t = own & (jnp.logical_not(inner) | (index < LATE))
                sub = half * HOPS + index
                x_way, x_slot = x_rest(x, half, index)
                relay_way = by_apart([max(place, 0) for place in places])
                from_way = pick(own, x_way, relay_way)
                from_slot = pick(own, x_slot, pick(apart == 2, own_slot(relay_index), slot))

            @pl.when(active & from_t)
            def _(way=way, slot=slot, sub=sub):
                send_own(way, slot, sub)

            @pl.when(active & jnp.logical_not(from_t))
            def _(way=way, slot=slot, from_way=from_way, from_slot=from_slot):
                landed(from_way, from_slot)
                send_on(way, slot, from_way, from_slot)

        return carry

    lax.fori_loop(0, HOPS + 2 * LAG, step, 0)

    @pl.when(jnp.logical_not(alone))
    def _():
        def finish(index, carry):
            for half in range(2):
                way, slot = landing(x, y, z, half, index)
                landed(way, slot)
                pltpu.make_async_copy(land.at[way, slot], m_buf.at[:, half * HOPS + index], m_sem).start()
            return carry

        lax.fori_loop(0, HOPS, finish, 0)
        pltpu.make_async_copy(m_buf, m_buf, m_sem).wait()

    @pl.when(alone)
    def _():
        swap(0).wait()
        swap(1).wait()
        pltpu.make_async_copy(t_ref.at[core], m_buf.at[core], m_sem).wait()


def drain_exchange(land, leave):
    def drain(slot, carry):
        for way in range(6):
            pltpu.make_async_copy(land.at[way, slot], land.at[way, slot], leave.at[way, slot]).wait()
        return carry

    lax.fori_loop(0, HOPS, drain, 0)


def cycle_kernel(
    t_ref, w_ref, mask_ref, land, out_ref,
    t_buf, m_buf, w_buf, o_buf, ring, relay, inbox,
    arrive, leave, t_sem, m_sem, w_sem, swap_arrive, swap_leave,
    ring_arrive, ring_leave, relay_arrive, relay_leave, inbox_arrive, inbox_leave,
):
    ring_sems, relay_sems, inbox_sems = (ring_arrive, ring_leave), (relay_arrive, relay_leave), (inbox_arrive, inbox_leave)
    x, y, z, core = position()
    slots, blocks, virtuals = w_buf.shape[0], w_buf.shape[1], w_buf.shape[2]

    barrier = pltpu.get_barrier_semaphore()
    for way in range(6):
        for other in range(2):
            pl.semaphore_signal(
                barrier, inc=1, device_id=device(*towards(x, y, z, way), other), device_id_type=MESH
            )
    pl.semaphore_signal(barrier, inc=1, device_id=device(x, y, z, 1 - core), device_id_type=MESH)
    pl.semaphore_wait(barrier, 13)

    load_t = pltpu.make_async_copy(t_ref, t_buf, t_sem)
    load_w = pltpu.make_async_copy(w_ref, w_buf, w_sem)
    load_t.start()
    load_w.start()

    exchange(t_ref, land, m_buf, arrive, leave, m_sem, swap_arrive, swap_leave)

    load_t.wait()
    load_w.wait()
    tiles = 8
    tile = virtuals // tiles

    def mask_band(n, carry):
        s, block, r = n // (blocks * tiles), (n // tiles) % blocks, n % tiles
        band = pl.ds(pl.multiple_of(r * tile, tile), tile)
        for c in range(tiles):
            keep = mask_ref[n * tiles + c]
            columns = pl.ds(c * tile, tile)
            value = w_buf[s, block, band, columns]
            w_buf[s, block, band, columns] = jnp.where(keep != 0, value, jnp.zeros_like(value))
        return carry

    lax.fori_loop(0, slots * blocks * tiles, mask_band, 0)

    x_half = x // 2
    half = BAND // 2
    wide = virtuals // 2

    def band_of(s, k):
        return pick(s == 0, y + SIDE - 1 - k, y + 1 + k) % SIDE

    def block_of(s, k, chunk, side):
        offset = pick(chunk == 0, 1 - x_half, x_half) * half
        rows = pl.ds(pl.multiple_of(band_of(s, k) * BAND + offset, half), half)
        return o_buf.at[s, rows, pl.ds(side * wide, wide)]

    def y_beside(s):
        return device(x, (y + pick(s == 0, 1, SIDE - 1)) % SIDE, z, core)

    def x_beside(s):
        return device((x + pick(s == 0, 1, SIDE - 1)) % SIDE, y, z, core)

    def remote(source, target, sems, at, where):
        return pltpu.make_async_remote_copy(
            src_ref=source,
            dst_ref=target,
            send_sem=sems[1].at[at],
            recv_sem=sems[0].at[at],
            device_id=where,
            device_id_type=MESH,
        )

    def ring_copy(s, k, chunk):
        return remote(block_of(s, k, chunk, 0), ring.at[s, k, chunk], ring_sems, (s, k, chunk), y_beside(s))

    def last_relay(s):
        return remote(block_of(s, 3, 0, 0), relay.at[s, SIDE], relay_sems, (s, SIDE), x_beside(s))

    def relay_copy(s, k):
        return remote(block_of(s, k, 0, 1), relay.at[s, k], relay_sems, (s, k), x_beside(s))

    def pass_on(s, k):
        relay_copy(s, k).wait_recv()
        inbox_copy(s, k).start()

    def inbox_copy(s, k):
        return remote(relay.at[s, k], inbox.at[s, k], inbox_sems, (s, k), x_beside(s))

    def late_copy(s, k):
        return remote(block_of(s, k, 1, 1), ring.at[s, k, 2], ring_sems, (s, k, 2), y_beside(s))

    def add_left(s, k, chunk):
        ring_copy(s, k - 1, chunk).wait_recv()
        block = block_of(s, k, chunk, 0)
        block[...] = block[...] + ring[s, k - 1, chunk]

    def turn_left(s, k, chunk):
        add_left(s, k, chunk)
        ring_copy(s, k, chunk).start()

    def turn_right(s, k):
        inbox_copy(s, k).wait_recv()
        block = block_of(s, k, 1, 1)
        if k == 0:
            block[...] = block[...] + inbox[s, k]
        else:
            late_copy(s, k - 1).wait_recv()
            block[...] = block[...] + inbox[s, k] + ring[s, k - 1, 2]
        late_copy(s, k).start()

    def unit(u, carry):
        s = u % 2
        index = band_of(s, u // 2)
        band = pl.ds(pl.multiple_of(index * BAND, BAND), BAND)
        subs = BAND // t_buf.shape[2]
        total = jnp.zeros((2 * BAND, virtuals), jnp.float32)
        for block in range(blocks):
            mirrored = m_buf[block, :, :, band].reshape(virtuals, BAND).T
            mixed = 2.0 * t_buf[block, pl.ds(index * subs, subs)].reshape(BAND, virtuals) - mirrored
            high = mixed.astype(jnp.bfloat16)
            low = (mixed - high.astype(jnp.float32)).astype(jnp.bfloat16)
            pair = jnp.concatenate([high, low], axis=0)
            total += jnp.dot(pair, w_buf[s, block], preferred_element_type=jnp.float32)
        o_buf[s, band, :] = total[:BAND] + total[BAND:]
        relay_copy(s, u // 2).start()

        @pl.when(u < 2)
        def _():
            ring_copy(s, 0, 0).start()
            ring_copy(s, 0, 1).start()

        @pl.when((u == 2) | (u == 3))
        def _():
            pass_on(s, 0)

        @pl.when(u == 3)
        def _():
            turn_left(0, 1, 0)
            turn_left(1, 1, 0)

        @pl.when(u == 4)
        def _():
            turn_left(0, 1, 1)
            turn_left(1, 1, 1)

        @pl.when((u == 5) | (u == 6))
        def _():
            pass_on(1 - s, 1)
            turn_right(1 - s, 0)

        @pl.when(u == 6)
        def _():
            turn_left(0, 2, 0)
            turn_left(1, 2, 0)

        return carry

    lax.fori_loop(0, slots * SIDE, unit, 0)

    def both(step, *arguments):
        for s in range(2):
            step(s, *arguments)

    both(turn_left, 2, 1)
    both(pass_on, 2)
    both(turn_right, 1)
    for s in range(2):
        add_left(s, 3, 0)
        last_relay(s).start()
    both(pass_on, 3)
    both(turn_right, 2)
    both(add_left, 3, 1)
    for s in range(2):
        last_relay(s).wait_recv()
        inbox_copy(s, SIDE).start()
    for s in range(2):
        inbox_copy(s, 3).wait_recv()
        late_copy(s, 2).wait_recv()
        out_ref[s, :, wide:] = block_of(s, 3, 1, 1)[...] + inbox[s, 3] + ring[s, 2, 2]
    for s in range(2):
        inbox_copy(s, SIDE).wait_recv()
        out_ref[s, :, :wide] = block_of(s, 3, 1, 0)[...] + inbox[s, SIDE]

    for s in range(2):
        for k in range(3):
            ring_copy(s, k, 0).wait_send()
            ring_copy(s, k, 1).wait_send()
            late_copy(s, k).wait_send()
        for k in range(SIDE):
            relay_copy(s, k).wait_send()
            inbox_copy(s, k).wait_send()
        last_relay(s).wait_send()
        inbox_copy(s, SIDE).wait_send()
    drain_exchange(land, leave)


def summed_rows(amplitudes, integrals, tile_mask):
    slots, blocks, virtuals = integrals.shape[0], integrals.shape[1], integrals.shape[2]
    rows = virtuals // SUBS
    half, wide = BAND // 2, virtuals // 2
    dma = pltpu.SemaphoreType.DMA
    return pl.pallas_call(
        cycle_kernel,
        out_shape=(
            jax.ShapeDtypeStruct((6, HOPS, blocks, rows, virtuals), jnp.float32),
            jax.ShapeDtypeStruct((slots, BAND // 2, virtuals), jnp.float32),
        ),
        in_specs=[HBM, HBM, pl.BlockSpec(memory_space=pltpu.SMEM)],
        out_specs=(HBM, pl.BlockSpec(memory_space=pltpu.VMEM)),
        scratch_shapes=[
            pltpu.VMEM((blocks, SUBS, rows, virtuals), jnp.float32),
            pltpu.VMEM((blocks, SUBS, rows, virtuals), jnp.float32),
            pltpu.VMEM((slots, blocks, virtuals, virtuals), jnp.bfloat16),
            pltpu.VMEM((slots, virtuals, virtuals), jnp.float32),
            pltpu.VMEM((slots, 3, 3, half, wide), jnp.float32),
            pltpu.VMEM((slots, SIDE + 1, half, wide), jnp.float32),
            pltpu.VMEM((slots, SIDE + 1, half, wide), jnp.float32),
            dma((6, HOPS)),
            dma((6, HOPS)),
            dma,
            dma,
            dma,
            dma((2,)),
            dma((2,)),
            dma((slots, 3, 3)),
            dma((slots, 3, 3)),
            dma((slots, SIDE + 1)),
            dma((slots, SIDE + 1)),
            dma((slots, SIDE + 1)),
            dma((slots, SIDE + 1)),
        ],
        compiler_params=pltpu.CompilerParams(
            collective_id=0, has_side_effects=True, vmem_limit_bytes=58 << 20
        ),
    )(amplitudes.reshape(blocks, SUBS, rows, virtuals), integrals, tile_mask.reshape(-1))[1]


def body(amplitudes, integrals, tile_mask, pair_list):
    own_rows = summed_rows(amplitudes[0], integrals[0], tile_mask[0])
    row_groups, col_groups = lax.axis_size("ia"), lax.axis_size("ka")
    slots, rows, virtuals = own_rows.shape
    thin, wide = rows // row_groups, virtuals // col_groups
    pieces = own_rows.reshape(slots, row_groups, thin, col_groups, wide).transpose(1, 3, 0, 2, 4)
    pieces = pieces.reshape(row_groups * col_groups, slots, thin, wide)
    spread = lax.all_to_all(pieces, ("ia", "ka"), split_axis=0, concat_axis=0, tiled=True)
    spread = spread.reshape(row_groups, col_groups, slots, thin, wide).transpose(0, 2, 1, 3, 4)
    spread = spread.reshape(row_groups * slots, col_groups, thin, wide)
    owners = jnp.arange(row_groups, dtype=jnp.int32)
    partner_slot = jnp.where(pair_list[pair_list, 0] == owners[:, None], 0, 1).astype(jnp.int32)
    source_row = pair_list * 2 + partner_slot
    routed = jnp.take(spread, source_row.reshape(-1), axis=0)
    routed = routed.reshape(row_groups, slots, col_groups, thin, wide)
    delivered = lax.all_to_all(routed, "ia", split_axis=0, concat_axis=0, tiled=True)
    mirrored = delivered.transpose(1, 4, 2, 0, 3).reshape(slots, wide, virtuals)
    return (own_rows + mirrored)[None]


def solution(mesh):
    placed = (
        P("ia", "ka", None, None),
        P("ia", None, "ka", None, None),
        P("ia", None, "ka", None, None),
        P(),
    )
    return jax.shard_map(
        body, mesh=mesh, in_specs=placed, out_specs=P("ia", None, "ka", None), check_vma=False
    )
```

```python
import jax
import jax.numpy as jnp
from jax import lax
from jax.experimental import pallas as pl
from jax.experimental.pallas import tpu as pltpu
from jax.sharding import PartitionSpec as P

MESH = pl.DeviceIdType.MESH
HBM = pl.BlockSpec(memory_space=pl.ANY)

SIDE = 4
STEPS = ((1, 0, 0), (-1, 0, 0), (0, 1, 0), (0, -1, 0), (0, 0, 1), (0, 0, -1))
HOPS = 32
LAG = 2
MASK_FROM = 4
LATE = HOPS // 2
SUBS = 2 * HOPS
CROSS_OWN = 3
BAND = 256


def position():
    ia, ka = lax.axis_index("ia"), lax.axis_index("ka")
    return (ka % 2) * 2 + (ia // 2) % 2, ka // 2, ia // 4, ia % 2


def towards(x, y, z, way):
    dx, dy, dz = STEPS[way]
    return (x + dx + SIDE) % SIDE, (y + dy + SIDE) % SIDE, (z + dz + SIDE) % SIDE


def device(x, y, z, core):
    return z * 4 + (x % 2) * 2 + core, y * 2 + x // 2


def pick(test, then, other):
    return jnp.where(test, then, other)


def own_slot(index):
    return pick(index < CROSS_OWN, index, 2 * index - 2)


def relay_slot(index):
    return pick(index > HOPS // 2 - 3, index + HOPS // 2, 2 * index + 3)


def yz_rest(y, z, half, index):
    apart = (z - y + SIDE) % SIDE
    even = index % 2 == 0
    two_way = pick(half == 0, pick(even, 4, 5), pick(even, 2, 3))
    way = pick(apart == 1, pick(half == 0, 4, 3), pick(apart == 3, pick(half == 0, 5, 2), two_way))
    return way, pick(apart == 2, relay_slot(index // 2), index)


def x_rest(x, half, index):
    return pick(half == 0, 2 - x, x - 1), (index + LATE) % HOPS


def landing(x, y, z, half, index):
    inner = (x == 1) | (x == 2)
    by_x = inner & ((index < LATE) | (y == z))
    way, slot = yz_rest(y, z, half, index)
    x_way, x_slot = x_rest(x, half, index)
    return pick(by_x, x_way, way), pick(by_x, x_slot, slot)


def exchange(t_ref, land, m_buf, arrive, leave, m_sem, swap_arrive, swap_leave, work):
    x, y, z, core = position()
    inner = (x == 1) | (x == 2)
    apart = (z - y + SIDE) % SIDE
    alone = (apart == 0) & jnp.logical_not(inner)

    def swap(half):
        return pltpu.make_async_remote_copy(
            src_ref=t_ref.at[1 - core, pl.ds(half * HOPS, HOPS)],
            dst_ref=m_buf.at[core, pl.ds(half * HOPS, HOPS)],
            send_sem=swap_leave.at[half],
            recv_sem=swap_arrive.at[half],
            device_id=device(x, y, z, 1 - core),
            device_id_type=MESH,
        )

    @pl.when(alone)
    def _():
        swap(0).start()
        swap(1).start()
        pltpu.make_async_copy(t_ref.at[core], m_buf.at[core], m_sem).start()

    def landed(way, slot):
        pltpu.make_async_copy(land.at[way, slot], land.at[way, slot], arrive.at[way, slot]).wait()

    def send_own(way, slot, sub):
        for block in range(2):
            pltpu.make_async_remote_copy(
                src_ref=t_ref.at[block, sub],
                dst_ref=land.at[way, slot, core],
                send_sem=leave.at[way, slot],
                recv_sem=arrive.at[way, slot],
                device_id=device(*towards(x, y, z, way), block),
                device_id_type=MESH,
            ).start()

    def send_on(way, slot, from_way, from_slot):
        pltpu.make_async_remote_copy(
            src_ref=land.at[from_way, from_slot],
            dst_ref=land.at[way, slot],
            send_sem=leave.at[way, slot],
            recv_sem=arrive.at[way, slot],
            device_id=device(*towards(x, y, z, way), core),
            device_id_type=MESH,
        ).start()

    relay_from = {2: (5, -1, 4, 4), 3: (4, 5, 5, -1), 4: (3, 2, 2, -1), 5: (2, -1, 3, 3)}

    def by_apart(values):
        zero, one, two, three = values
        return pick(apart == 0, zero, pick(apart == 1, one, pick(apart == 2, two, three)))

    def yz_lag(way):
        return by_apart([0 if source < 0 or place == 2 else LAG for place, source in enumerate(relay_from[way])])

    lags = [
        pick(inner, 0, pick(x == 3, LAG, 2 * LAG)),
        pick(inner, 0, pick(x == 0, LAG, 2 * LAG)),
    ] + [yz_lag(way) for way in range(2, 6)]

    def step(t, carry):
        for way in range(6):
            slot = t - lags[way]
            active = (slot >= 0) & (slot < HOPS)
            if way < 2:
                half = pick(x == 1 + way, 0, 1)
                index = (slot + LATE) % HOPS
                from_t = inner & ((slot < LATE) | (apart == 0))
                sub = half * HOPS + index
                rest_way, rest_slot = yz_rest(y, z, half, index)
                from_way, from_slot = pick(inner, rest_way, way), pick(inner, rest_slot, slot)
            else:
                half = 0 if way < 4 else 1
                odd = way % 2
                early, late = slot < CROSS_OWN, slot > HOPS - 3
                relayed = late | (jnp.logical_not(early) & (slot % 2 == 1))
                own_index = pick(early, slot, (slot + 2) // 2)
                relay_index = pick(late, slot - HOPS // 2, (slot - 3) // 2)
                index = pick(apart == 2, 2 * own_index + odd, slot)
                places = relay_from[way]
                near_own = by_apart([places[0] < 0, places[1] < 0, False, places[3] < 0])
                own = pick(apart == 2, jnp.logical_not(relayed), near_own)
                from_t = own & (jnp.logical_not(inner) | (index < LATE))
                sub = half * HOPS + index
                x_way, x_slot = x_rest(x, half, index)
                relay_way = by_apart([max(place, 0) for place in places])
                from_way = pick(own, x_way, relay_way)
                from_slot = pick(own, x_slot, pick(apart == 2, own_slot(relay_index), slot))

            @pl.when(active & from_t)
            def _(way=way, slot=slot, sub=sub):
                send_own(way, slot, sub)

            @pl.when(active & jnp.logical_not(from_t))
            def _(way=way, slot=slot, from_way=from_way, from_slot=from_slot):
                landed(from_way, from_slot)
                send_on(way, slot, from_way, from_slot)

        work(t)
        return carry

    lax.fori_loop(0, HOPS + 2 * LAG, step, 0)

    @pl.when(jnp.logical_not(alone))
    def _():
        def finish(index, carry):
            for half in range(2):
                way, slot = landing(x, y, z, half, index)
                landed(way, slot)
                pltpu.make_async_copy(land.at[way, slot], m_buf.at[:, half * HOPS + index], m_sem).start()
            return carry

        lax.fori_loop(0, HOPS, finish, 0)
        pltpu.make_async_copy(m_buf, m_buf, m_sem).wait()

    @pl.when(alone)
    def _():
        swap(0).wait()
        swap(1).wait()
        pltpu.make_async_copy(t_ref.at[core], m_buf.at[core], m_sem).wait()


def drain_exchange(land, leave):
    def drain(slot, carry):
        for way in range(6):
            pltpu.make_async_copy(land.at[way, slot], land.at[way, slot], leave.at[way, slot]).wait()
        return carry

    lax.fori_loop(0, HOPS, drain, 0)


def cycle_kernel(
    t_ref, w_ref, mask_ref, land, out_ref, spread,
    t_buf, m_buf, w_buf, o_buf, ring, relay, inbox,
    arrive, leave, t_sem, m_sem, w_sem, swap_arrive, swap_leave,
    ring_arrive, ring_leave, relay_arrive, relay_leave, inbox_arrive, inbox_leave,
    spread_arrive, spread_leave,
):
    ring_sems, relay_sems, inbox_sems = (ring_arrive, ring_leave), (relay_arrive, relay_leave), (inbox_arrive, inbox_leave)
    x, y, z, core = position()
    slots, blocks, virtuals = w_buf.shape[0], w_buf.shape[1], w_buf.shape[2]

    row_groups, col_groups = lax.axis_size("ia"), lax.axis_size("ka")
    devices = row_groups * col_groups
    row, col = lax.axis_index("ia"), lax.axis_index("ka")
    barrier = pltpu.get_barrier_semaphore()

    def greet(n, carry):
        other = (row * col_groups + col + n) % devices
        pl.semaphore_signal(
            barrier, inc=1, device_id=(other // col_groups, other % col_groups), device_id_type=MESH
        )
        return carry

    lax.fori_loop(1, devices, greet, 0)
    pl.semaphore_wait(barrier, devices - 1)

    load_t = pltpu.make_async_copy(t_ref, t_buf, t_sem)
    load_w = pltpu.make_async_copy(w_ref, w_buf, w_sem)
    load_t.start()
    load_w.start()

    tiles = 8
    tile = virtuals // tiles

    def mask_band(n):
        s, block, r = n // (blocks * tiles), (n // tiles) % blocks, n % tiles
        band = pl.ds(pl.multiple_of(r * tile, tile), tile)
        for c in range(tiles):
            keep = mask_ref[s, block, r, c]
            columns = pl.ds(c * tile, tile)
            value = w_buf[s, block, band, columns]
            w_buf[s, block, band, columns] = jnp.where(keep != 0, value, jnp.zeros_like(value))

    def work(t):
        @pl.when(t == MASK_FROM)
        def _():
            load_t.wait()
            load_w.wait()

        @pl.when((t >= MASK_FROM) & (t < MASK_FROM + slots * blocks * tiles // 2))
        def _():
            mask_band(2 * (t - MASK_FROM))
            mask_band(2 * (t - MASK_FROM) + 1)

    exchange(t_ref, land, m_buf, arrive, leave, m_sem, swap_arrive, swap_leave, work)

    x_half = x // 2
    half = BAND // 2
    wide = virtuals // 2

    def band_of(s, k):
        return pick(s == 0, y + SIDE - 1 - k, y + 1 + k) % SIDE

    def block_of(s, k, chunk, side):
        offset = pick(chunk == 0, 1 - x_half, x_half) * half
        rows = pl.ds(pl.multiple_of(band_of(s, k) * BAND + offset, half), half)
        return o_buf.at[s, rows, pl.ds(side * wide, wide)]

    def y_beside(s):
        return device(x, (y + pick(s == 0, 1, SIDE - 1)) % SIDE, z, core)

    def x_beside(s):
        return device((x + pick(s == 0, 1, SIDE - 1)) % SIDE, y, z, core)

    def remote(source, target, sems, at, where):
        return pltpu.make_async_remote_copy(
            src_ref=source,
            dst_ref=target,
            send_sem=sems[1].at[at],
            recv_sem=sems[0].at[at],
            device_id=where,
            device_id_type=MESH,
        )

    def ring_copy(s, k, chunk):
        return remote(block_of(s, k, chunk, 0), ring.at[s, k, chunk], ring_sems, (s, k, chunk), y_beside(s))

    def last_relay(s):
        return remote(block_of(s, 3, 0, 0), relay.at[s, SIDE], relay_sems, (s, SIDE), x_beside(s))

    def relay_copy(s, k):
        return remote(block_of(s, k, 0, 1), relay.at[s, k], relay_sems, (s, k), x_beside(s))

    def pass_on(s, k):
        relay_copy(s, k).wait_recv()
        inbox_copy(s, k).start()

    def inbox_copy(s, k):
        return remote(relay.at[s, k], inbox.at[s, k], inbox_sems, (s, k), x_beside(s))

    def late_copy(s, k):
        return remote(block_of(s, k, 1, 1), ring.at[s, k, 2], ring_sems, (s, k, 2), y_beside(s))

    def add_left(s, k, chunk):
        ring_copy(s, k - 1, chunk).wait_recv()
        block = block_of(s, k, chunk, 0)
        block[...] = block[...] + ring[s, k - 1, chunk]

    def turn_left(s, k, chunk):
        add_left(s, k, chunk)
        ring_copy(s, k, chunk).start()

    def turn_right(s, k):
        inbox_copy(s, k).wait_recv()
        block = block_of(s, k, 1, 1)
        if k == 0:
            block[...] = block[...] + inbox[s, k]
        else:
            late_copy(s, k - 1).wait_recv()
            block[...] = block[...] + inbox[s, k] + ring[s, k - 1, 2]
        late_copy(s, k).start()

    def unit(u, carry):
        s = u % 2
        index = band_of(s, u // 2)
        band = pl.ds(pl.multiple_of(index * BAND, BAND), BAND)
        subs = BAND // t_buf.shape[2]
        total = jnp.zeros((2 * BAND, virtuals), jnp.float32)
        for block in range(blocks):
            mirrored = m_buf[block, :, :, band].reshape(virtuals, BAND).T
            mixed = 2.0 * t_buf[block, pl.ds(index * subs, subs)].reshape(BAND, virtuals) - mirrored
            high = mixed.astype(jnp.bfloat16)
            low = (mixed - high.astype(jnp.float32)).astype(jnp.bfloat16)
            pair = jnp.concatenate([high, low], axis=0)
            total += jnp.dot(pair, w_buf[s, block], preferred_element_type=jnp.float32)
        o_buf[s, band, :] = total[:BAND] + total[BAND:]
        relay_copy(s, u // 2).start()

        @pl.when(u < 2)
        def _():
            ring_copy(s, 0, 0).start()
            ring_copy(s, 0, 1).start()

        @pl.when((u == 2) | (u == 3))
        def _():
            pass_on(s, 0)

        @pl.when(u == 3)
        def _():
            turn_left(0, 1, 0)
            turn_left(1, 1, 0)

        @pl.when(u == 4)
        def _():
            turn_left(0, 1, 1)
            turn_left(1, 1, 1)

        @pl.when((u == 5) | (u == 6))
        def _():
            pass_on(1 - s, 1)
            turn_right(1 - s, 0)

        @pl.when(u == 6)
        def _():
            turn_left(0, 2, 0)
            turn_left(1, 2, 0)

        return carry

    lax.fori_loop(0, slots * SIDE, unit, 0)

    def both(step, *arguments):
        for s in range(2):
            step(s, *arguments)

    both(turn_left, 2, 1)
    both(pass_on, 2)
    both(turn_right, 1)
    for s in range(2):
        add_left(s, 3, 0)
        last_relay(s).start()
    both(pass_on, 3)
    both(turn_right, 2)
    both(add_left, 3, 1)
    for s in range(2):
        last_relay(s).wait_recv()
        inbox_copy(s, SIDE).start()
    thin, slim = half // row_groups, virtuals // col_groups

    def piece_of(to_row, to_col):
        rows = pl.ds(pl.multiple_of(to_row * thin, thin), thin)
        columns = pl.ds(pl.multiple_of(to_col * slim, slim), slim)
        return out_ref.at[:, rows, columns]

    def scatter(side):
        span = col_groups // 2

        def send(n, carry):
            to_row = (row + n // span) % row_groups
            to_col = side * span + (col + n) % span
            target = spread.at[row * col_groups + col]

            @pl.when((to_row == row) & (to_col == col))
            def _():
                pltpu.make_async_copy(piece_of(to_row, to_col), target, spread_arrive).start()

            @pl.when((to_row != row) | (to_col != col))
            def _():
                pltpu.make_async_remote_copy(
                    src_ref=piece_of(to_row, to_col),
                    dst_ref=target,
                    send_sem=spread_leave,
                    recv_sem=spread_arrive,
                    device_id=(to_row, to_col),
                    device_id_type=MESH,
                ).start()

            return carry

        lax.fori_loop(0, row_groups * span, send, 0)

    for s in range(2):
        inbox_copy(s, 3).wait_recv()
        late_copy(s, 2).wait_recv()
        out_ref[s, :, wide:] = block_of(s, 3, 1, 1)[...] + inbox[s, 3] + ring[s, 2, 2]
    scatter(1)
    for s in range(2):
        inbox_copy(s, SIDE).wait_recv()
        out_ref[s, :, :wide] = block_of(s, 3, 1, 0)[...] + inbox[s, SIDE]
    scatter(0)

    for s in range(2):
        for k in range(3):
            ring_copy(s, k, 0).wait_send()
            ring_copy(s, k, 1).wait_send()
            late_copy(s, k).wait_send()
        for k in range(SIDE):
            relay_copy(s, k).wait_send()
            inbox_copy(s, k).wait_send()
        last_relay(s).wait_send()
        inbox_copy(s, SIDE).wait_send()
    drain_exchange(land, leave)
    sent = spread.at[pl.ds(0, devices - 1)]
    pltpu.make_async_copy(sent, sent, spread_leave).wait()
    pltpu.make_async_copy(spread, spread, spread_arrive).wait()


def summed_rows(amplitudes, integrals, tile_mask):
    slots, blocks, virtuals = integrals.shape[0], integrals.shape[1], integrals.shape[2]
    rows = virtuals // SUBS
    half, wide = BAND // 2, virtuals // 2
    dma = pltpu.SemaphoreType.DMA
    row_groups, col_groups = lax.axis_size("ia"), lax.axis_size("ka")
    devices = row_groups * col_groups
    return pl.pallas_call(
        cycle_kernel,
        out_shape=(
            jax.ShapeDtypeStruct((6, HOPS, blocks, rows, virtuals), jnp.float32),
            jax.ShapeDtypeStruct((slots, half, virtuals), jnp.float32),
            jax.ShapeDtypeStruct((devices, slots, half // row_groups, virtuals // col_groups), jnp.float32),
        ),
        in_specs=[HBM, HBM, pl.BlockSpec(memory_space=pltpu.SMEM)],
        out_specs=(HBM, pl.BlockSpec(memory_space=pltpu.VMEM), HBM),
        scratch_shapes=[
            pltpu.VMEM((blocks, SUBS, rows, virtuals), jnp.float32),
            pltpu.VMEM((blocks, SUBS, rows, virtuals), jnp.float32),
            pltpu.VMEM((slots, blocks, virtuals, virtuals), jnp.bfloat16),
            pltpu.VMEM((slots, virtuals, virtuals), jnp.float32),
            pltpu.VMEM((slots, 3, 3, half, wide), jnp.float32),
            pltpu.VMEM((slots, SIDE + 1, half, wide), jnp.float32),
            pltpu.VMEM((slots, SIDE + 1, half, wide), jnp.float32),
            dma((6, HOPS)),
            dma((6, HOPS)),
            dma,
            dma,
            dma,
            dma((2,)),
            dma((2,)),
            dma((slots, 3, 3)),
            dma((slots, 3, 3)),
            dma((slots, SIDE + 1)),
            dma((slots, SIDE + 1)),
            dma((slots, SIDE + 1)),
            dma((slots, SIDE + 1)),
            dma,
            dma,
        ],
        compiler_params=pltpu.CompilerParams(
            collective_id=0, has_side_effects=True, vmem_limit_bytes=58 << 20
        ),
    )(amplitudes.reshape(blocks, SUBS, rows, virtuals), integrals, tile_mask)[1:]


def body(amplitudes, integrals, tile_mask, pair_list):
    own_rows, spread = summed_rows(amplitudes[0], integrals[0], tile_mask[0])
    row_groups, col_groups = lax.axis_size("ia"), lax.axis_size("ka")
    slots, rows, virtuals = own_rows.shape
    thin, wide = rows // row_groups, virtuals // col_groups
    spread = spread.reshape(row_groups, col_groups, slots, thin, wide).transpose(0, 2, 1, 3, 4)
    spread = spread.reshape(row_groups * slots, col_groups, thin, wide)
    owners = jnp.arange(row_groups, dtype=jnp.int32)
    partner_slot = jnp.where(pair_list[pair_list, 0] == owners[:, None], 0, 1).astype(jnp.int32)
    source_row = pair_list * 2 + partner_slot
    routed = jnp.take(spread, source_row.reshape(-1), axis=0)
    routed = routed.reshape(row_groups, slots, col_groups, thin, wide)
    delivered = lax.all_to_all(routed, "ia", split_axis=0, concat_axis=0, tiled=True)
    mirrored = delivered.transpose(1, 4, 2, 0, 3).reshape(slots, wide, virtuals)
    return (own_rows + mirrored)[None]


def solution(mesh):
    placed = (
        P("ia", "ka", None, None),
        P("ia", None, "ka", None, None),
        P("ia", None, "ka", None, None),
        P(),
    )
    return jax.shard_map(
        body, mesh=mesh, in_specs=placed, out_specs=P("ia", None, "ka", None), check_vma=False
    )
```

```python
import jax
import jax.numpy as jnp
from jax import lax
from jax.experimental import pallas as pl
from jax.experimental.pallas import tpu as pltpu
from jax.sharding import PartitionSpec as P

MESH = pl.DeviceIdType.MESH
HBM = pl.BlockSpec(memory_space=pl.ANY)

SIDE = 4
STEPS = ((1, 0, 0), (-1, 0, 0), (0, 1, 0), (0, -1, 0), (0, 0, 1), (0, 0, -1))
HOPS = 32
LAG = 2
MASK_FROM = 4
LATE = HOPS // 2
SUBS = 2 * HOPS
CROSS_OWN = 3
BAND = 256


def position():
    ia, ka = lax.axis_index("ia"), lax.axis_index("ka")
    return (ka % 2) * 2 + (ia // 2) % 2, ka // 2, ia // 4, ia % 2


def towards(x, y, z, way):
    dx, dy, dz = STEPS[way]
    return (x + dx + SIDE) % SIDE, (y + dy + SIDE) % SIDE, (z + dz + SIDE) % SIDE


def device(x, y, z, core):
    return z * 4 + (x % 2) * 2 + core, y * 2 + x // 2


def pick(test, then, other):
    return jnp.where(test, then, other)


def own_slot(index):
    return pick(index < CROSS_OWN, index, 2 * index - 2)


def relay_slot(index):
    return pick(index > HOPS // 2 - 3, index + HOPS // 2, 2 * index + 3)


def yz_rest(y, z, half, index):
    apart = (z - y + SIDE) % SIDE
    even = index % 2 == 0
    two_way = pick(half == 0, pick(even, 4, 5), pick(even, 2, 3))
    way = pick(apart == 1, pick(half == 0, 4, 3), pick(apart == 3, pick(half == 0, 5, 2), two_way))
    return way, pick(apart == 2, relay_slot(index // 2), index)


def x_rest(x, half, index):
    return pick(half == 0, 2 - x, x - 1), (index + LATE) % HOPS


def landing(x, y, z, half, index):
    inner = (x == 1) | (x == 2)
    by_x = inner & ((index < LATE) | (y == z))
    way, slot = yz_rest(y, z, half, index)
    x_way, x_slot = x_rest(x, half, index)
    return pick(by_x, x_way, way), pick(by_x, x_slot, slot)


def exchange(t_ref, land, m_buf, arrive, leave, m_sem, swap_arrive, swap_leave, work):
    x, y, z, core = position()
    inner = (x == 1) | (x == 2)
    apart = (z - y + SIDE) % SIDE
    alone = (apart == 0) & jnp.logical_not(inner)

    def swap(half):
        return pltpu.make_async_remote_copy(
            src_ref=t_ref.at[1 - core, pl.ds(half * HOPS, HOPS)],
            dst_ref=m_buf.at[core, pl.ds(half * HOPS, HOPS)],
            send_sem=swap_leave.at[half],
            recv_sem=swap_arrive.at[half],
            device_id=device(x, y, z, 1 - core),
            device_id_type=MESH,
        )

    @pl.when(alone)
    def _():
        swap(0).start()
        swap(1).start()
        pltpu.make_async_copy(t_ref.at[core], m_buf.at[core], m_sem).start()

    def landed(way, slot):
        pltpu.make_async_copy(land.at[way, slot], land.at[way, slot], arrive.at[way, slot]).wait()

    def send_own(way, slot, sub):
        for block in range(2):
            pltpu.make_async_remote_copy(
                src_ref=t_ref.at[block, sub],
                dst_ref=land.at[way, slot, core],
                send_sem=leave.at[way, slot],
                recv_sem=arrive.at[way, slot],
                device_id=device(*towards(x, y, z, way), block),
                device_id_type=MESH,
            ).start()

    def send_on(way, slot, from_way, from_slot):
        pltpu.make_async_remote_copy(
            src_ref=land.at[from_way, from_slot],
            dst_ref=land.at[way, slot],
            send_sem=leave.at[way, slot],
            recv_sem=arrive.at[way, slot],
            device_id=device(*towards(x, y, z, way), core),
            device_id_type=MESH,
        ).start()

    relay_from = {2: (5, -1, 4, 4), 3: (4, 5, 5, -1), 4: (3, 2, 2, -1), 5: (2, -1, 3, 3)}

    def by_apart(values):
        zero, one, two, three = values
        return pick(apart == 0, zero, pick(apart == 1, one, pick(apart == 2, two, three)))

    def yz_lag(way):
        return by_apart([0 if source < 0 or place == 2 else LAG for place, source in enumerate(relay_from[way])])

    lags = [
        pick(inner, 0, pick(x == 3, LAG, 2 * LAG)),
        pick(inner, 0, pick(x == 0, LAG, 2 * LAG)),
    ] + [yz_lag(way) for way in range(2, 6)]

    def step(t, carry):
        for way in range(6):
            slot = t - lags[way]
            active = (slot >= 0) & (slot < HOPS)
            if way < 2:
                half = pick(x == 1 + way, 0, 1)
                index = (slot + LATE) % HOPS
                from_t = inner & ((slot < LATE) | (apart == 0))
                sub = half * HOPS + index
                rest_way, rest_slot = yz_rest(y, z, half, index)
                from_way, from_slot = pick(inner, rest_way, way), pick(inner, rest_slot, slot)
            else:
                half = 0 if way < 4 else 1
                odd = way % 2
                early, late = slot < CROSS_OWN, slot > HOPS - 3
                relayed = late | (jnp.logical_not(early) & (slot % 2 == 1))
                own_index = pick(early, slot, (slot + 2) // 2)
                relay_index = pick(late, slot - HOPS // 2, (slot - 3) // 2)
                index = pick(apart == 2, 2 * own_index + odd, slot)
                places = relay_from[way]
                near_own = by_apart([places[0] < 0, places[1] < 0, False, places[3] < 0])
                own = pick(apart == 2, jnp.logical_not(relayed), near_own)
                from_t = own & (jnp.logical_not(inner) | (index < LATE))
                sub = half * HOPS + index
                x_way, x_slot = x_rest(x, half, index)
                relay_way = by_apart([max(place, 0) for place in places])
                from_way = pick(own, x_way, relay_way)
                from_slot = pick(own, x_slot, pick(apart == 2, own_slot(relay_index), slot))

            @pl.when(active & from_t)
            def _(way=way, slot=slot, sub=sub):
                send_own(way, slot, sub)

            @pl.when(active & jnp.logical_not(from_t))
            def _(way=way, slot=slot, from_way=from_way, from_slot=from_slot):
                landed(from_way, from_slot)
                send_on(way, slot, from_way, from_slot)

        work(t)
        return carry

    lax.fori_loop(0, HOPS + 2 * LAG, step, 0)

    @pl.when(jnp.logical_not(alone))
    def _():
        def finish(index, carry):
            for half in range(2):
                way, slot = landing(x, y, z, half, index)
                landed(way, slot)
                pltpu.make_async_copy(land.at[way, slot], m_buf.at[:, half * HOPS + index], m_sem).start()
            return carry

        lax.fori_loop(0, HOPS, finish, 0)
        pltpu.make_async_copy(m_buf, m_buf, m_sem).wait()

    @pl.when(alone)
    def _():
        swap(0).wait()
        swap(1).wait()
        pltpu.make_async_copy(t_ref.at[core], m_buf.at[core], m_sem).wait()


def drain_exchange(land, leave):
    def drain(slot, carry):
        for way in range(6):
            pltpu.make_async_copy(land.at[way, slot], land.at[way, slot], leave.at[way, slot]).wait()
        return carry

    lax.fori_loop(0, HOPS, drain, 0)


def cycle_kernel(
    t_ref, w_ref, mask_ref, pair_ref, land, out_ref,
    t_buf, m_buf, w_buf, o_buf, ring, relay, inbox,
    arrive, leave, t_sem, m_sem, w_sem, swap_arrive, swap_leave,
    ring_arrive, ring_leave, relay_arrive, relay_leave, inbox_arrive, inbox_leave,
    own, spread, stage, final, spread_arrive, spread_leave, final_arrive, final_leave,
):
    ring_sems, relay_sems, inbox_sems = (ring_arrive, ring_leave), (relay_arrive, relay_leave), (inbox_arrive, inbox_leave)
    x, y, z, core = position()
    slots, blocks, virtuals = w_buf.shape[0], w_buf.shape[1], w_buf.shape[2]

    row_groups, col_groups = lax.axis_size("ia"), lax.axis_size("ka")
    devices = row_groups * col_groups
    row, col = lax.axis_index("ia"), lax.axis_index("ka")
    barrier = pltpu.get_barrier_semaphore()

    def greet(n, carry):
        other = (row * col_groups + col + n) % devices
        pl.semaphore_signal(
            barrier, inc=1, device_id=(other // col_groups, other % col_groups), device_id_type=MESH
        )
        return carry

    lax.fori_loop(1, devices, greet, 0)
    pl.semaphore_wait(barrier, devices - 1)

    load_t = pltpu.make_async_copy(t_ref, t_buf, t_sem)
    load_w = pltpu.make_async_copy(w_ref, w_buf, w_sem)
    load_t.start()
    load_w.start()

    tiles = 8
    tile = virtuals // tiles

    def mask_band(n):
        s, block, r = n // (blocks * tiles), (n // tiles) % blocks, n % tiles
        band = pl.ds(pl.multiple_of(r * tile, tile), tile)
        for c in range(tiles):
            keep = mask_ref[s, block, r, c]
            columns = pl.ds(c * tile, tile)
            value = w_buf[s, block, band, columns]
            w_buf[s, block, band, columns] = jnp.where(keep != 0, value, jnp.zeros_like(value))

    def work(t):
        @pl.when(t == MASK_FROM)
        def _():
            load_t.wait()
            load_w.wait()

        @pl.when((t >= MASK_FROM) & (t < MASK_FROM + slots * blocks * tiles // 2))
        def _():
            mask_band(2 * (t - MASK_FROM))
            mask_band(2 * (t - MASK_FROM) + 1)

    exchange(t_ref, land, m_buf, arrive, leave, m_sem, swap_arrive, swap_leave, work)

    x_half = x // 2
    half = BAND // 2
    wide = virtuals // 2

    def band_of(s, k):
        return pick(s == 0, y + SIDE - 1 - k, y + 1 + k) % SIDE

    def block_of(s, k, chunk, side):
        offset = pick(chunk == 0, 1 - x_half, x_half) * half
        rows = pl.ds(pl.multiple_of(band_of(s, k) * BAND + offset, half), half)
        return o_buf.at[s, rows, pl.ds(side * wide, wide)]

    def y_beside(s):
        return device(x, (y + pick(s == 0, 1, SIDE - 1)) % SIDE, z, core)

    def x_beside(s):
        return device((x + pick(s == 0, 1, SIDE - 1)) % SIDE, y, z, core)

    def remote(source, target, sems, at, where):
        return pltpu.make_async_remote_copy(
            src_ref=source,
            dst_ref=target,
            send_sem=sems[1].at[at],
            recv_sem=sems[0].at[at],
            device_id=where,
            device_id_type=MESH,
        )

    def ring_copy(s, k, chunk):
        return remote(block_of(s, k, chunk, 0), ring.at[s, k, chunk], ring_sems, (s, k, chunk), y_beside(s))

    def last_relay(s):
        return remote(block_of(s, 3, 0, 0), relay.at[s, SIDE], relay_sems, (s, SIDE), x_beside(s))

    def relay_copy(s, k):
        return remote(block_of(s, k, 0, 1), relay.at[s, k], relay_sems, (s, k), x_beside(s))

    def pass_on(s, k):
        relay_copy(s, k).wait_recv()
        inbox_copy(s, k).start()

    def inbox_copy(s, k):
        return remote(relay.at[s, k], inbox.at[s, k], inbox_sems, (s, k), x_beside(s))

    def late_copy(s, k):
        return remote(block_of(s, k, 1, 1), ring.at[s, k, 2], ring_sems, (s, k, 2), y_beside(s))

    def add_left(s, k, chunk):
        ring_copy(s, k - 1, chunk).wait_recv()
        block = block_of(s, k, chunk, 0)
        block[...] = block[...] + ring[s, k - 1, chunk]

    def turn_left(s, k, chunk):
        add_left(s, k, chunk)
        ring_copy(s, k, chunk).start()

    def turn_right(s, k):
        inbox_copy(s, k).wait_recv()
        block = block_of(s, k, 1, 1)
        if k == 0:
            block[...] = block[...] + inbox[s, k]
        else:
            late_copy(s, k - 1).wait_recv()
            block[...] = block[...] + inbox[s, k] + ring[s, k - 1, 2]
        late_copy(s, k).start()

    def unit(u, carry):
        s = u % 2
        index = band_of(s, u // 2)
        band = pl.ds(pl.multiple_of(index * BAND, BAND), BAND)
        subs = BAND // t_buf.shape[2]
        total = jnp.zeros((2 * BAND, virtuals), jnp.float32)
        for block in range(blocks):
            mirrored = m_buf[block, :, :, band].reshape(virtuals, BAND).T
            mixed = 2.0 * t_buf[block, pl.ds(index * subs, subs)].reshape(BAND, virtuals) - mirrored
            high = mixed.astype(jnp.bfloat16)
            low = (mixed - high.astype(jnp.float32)).astype(jnp.bfloat16)
            pair = jnp.concatenate([high, low], axis=0)
            total += jnp.dot(pair, w_buf[s, block], preferred_element_type=jnp.float32)
        o_buf[s, band, :] = total[:BAND] + total[BAND:]
        relay_copy(s, u // 2).start()

        @pl.when(u < 2)
        def _():
            ring_copy(s, 0, 0).start()
            ring_copy(s, 0, 1).start()

        @pl.when((u == 2) | (u == 3))
        def _():
            pass_on(s, 0)

        @pl.when(u == 3)
        def _():
            turn_left(0, 1, 0)
            turn_left(1, 1, 0)

        @pl.when(u == 4)
        def _():
            turn_left(0, 1, 1)
            turn_left(1, 1, 1)

        @pl.when((u == 5) | (u == 6))
        def _():
            pass_on(1 - s, 1)
            turn_right(1 - s, 0)

        @pl.when(u == 6)
        def _():
            turn_left(0, 2, 0)
            turn_left(1, 2, 0)

        return carry

    lax.fori_loop(0, slots * SIDE, unit, 0)

    def both(step, *arguments):
        for s in range(2):
            step(s, *arguments)

    both(turn_left, 2, 1)
    both(pass_on, 2)
    both(turn_right, 1)
    for s in range(2):
        add_left(s, 3, 0)
        last_relay(s).start()
    both(pass_on, 3)
    both(turn_right, 2)
    both(add_left, 3, 1)
    for s in range(2):
        last_relay(s).wait_recv()
        inbox_copy(s, SIDE).start()
    thin, slim = half // row_groups, virtuals // col_groups

    def piece_of(to_row, to_col):
        rows = pl.ds(pl.multiple_of(to_row * thin, thin), thin)
        columns = pl.ds(pl.multiple_of(to_col * slim, slim), slim)
        return own.at[:, rows, columns]

    def scatter(side):
        span = col_groups // 2

        def send(n, carry):
            to_row = (row + n // span) % row_groups
            to_col = side * span + (col + n) % span
            target = spread.at[row * col_groups + col]

            @pl.when((to_row == row) & (to_col == col))
            def _():
                pltpu.make_async_copy(piece_of(to_row, to_col), target, spread_arrive).start()

            @pl.when((to_row != row) | (to_col != col))
            def _():
                pltpu.make_async_remote_copy(
                    src_ref=piece_of(to_row, to_col),
                    dst_ref=target,
                    send_sem=spread_leave,
                    recv_sem=spread_arrive,
                    device_id=(to_row, to_col),
                    device_id_type=MESH,
                ).start()

            return carry

        lax.fori_loop(0, row_groups * span, send, 0)

    for s in range(2):
        inbox_copy(s, 3).wait_recv()
        late_copy(s, 2).wait_recv()
        own[s, :, wide:] = block_of(s, 3, 1, 1)[...] + inbox[s, 3] + ring[s, 2, 2]
    scatter(1)
    for s in range(2):
        inbox_copy(s, SIDE).wait_recv()
        own[s, :, :wide] = block_of(s, 3, 1, 0)[...] + inbox[s, SIDE]
    scatter(0)
    pltpu.make_async_copy(spread, spread, spread_arrive).wait()

    def route(i, carry):
        for s in range(slots):
            j = pair_ref[s, i]
            t = jnp.where(pair_ref[0, j] == i, 0, 1)
            for k in range(col_groups):
                stage[i, s, k] = spread[j * col_groups + k, t]
        return carry

    lax.fori_loop(0, row_groups, route, 0)
    pltpu.make_async_copy(stage.at[row], final.at[row], final_arrive).start()

    def deliver(n, carry):
        to_row = (row + n) % row_groups
        pltpu.make_async_remote_copy(
            src_ref=stage.at[to_row],
            dst_ref=final.at[row],
            send_sem=final_leave,
            recv_sem=final_arrive,
            device_id=(to_row, col),
            device_id_type=MESH,
        ).start()
        return carry

    lax.fori_loop(1, row_groups, deliver, 0)

    for s in range(2):
        for k in range(3):
            ring_copy(s, k, 0).wait_send()
            ring_copy(s, k, 1).wait_send()
            late_copy(s, k).wait_send()
        for k in range(SIDE):
            relay_copy(s, k).wait_send()
            inbox_copy(s, k).wait_send()
        last_relay(s).wait_send()
        inbox_copy(s, SIDE).wait_send()
    drain_exchange(land, leave)
    sent = spread.at[pl.ds(0, devices - 1)]
    pltpu.make_async_copy(sent, sent, spread_leave).wait()

    pltpu.make_async_copy(final, final, final_arrive).wait()
    for s in range(slots):
        for k in range(col_groups):
            columns = pl.ds(k * half, half)
            out_ref[s, :, columns] = own[s, :, columns] + final[:, s, k].reshape(half, slim).T
    delivered = final.at[pl.ds(0, row_groups - 1)]
    pltpu.make_async_copy(delivered, delivered, final_leave).wait()


def residual_rows(amplitudes, integrals, tile_mask, pair_list):
    slots, blocks, virtuals = integrals.shape[0], integrals.shape[1], integrals.shape[2]
    rows = virtuals // SUBS
    half, wide = BAND // 2, virtuals // 2
    dma = pltpu.SemaphoreType.DMA
    row_groups, col_groups = lax.axis_size("ia"), lax.axis_size("ka")
    devices = row_groups * col_groups
    thin, slim = half // row_groups, virtuals // col_groups
    return pl.pallas_call(
        cycle_kernel,
        out_shape=(
            jax.ShapeDtypeStruct((6, HOPS, blocks, rows, virtuals), jnp.float32),
            jax.ShapeDtypeStruct((slots, half, virtuals), jnp.float32),
        ),
        in_specs=[HBM, HBM, pl.BlockSpec(memory_space=pltpu.SMEM), pl.BlockSpec(memory_space=pltpu.SMEM)],
        out_specs=(HBM, pl.BlockSpec(memory_space=pltpu.VMEM)),
        scratch_shapes=[
            pltpu.VMEM((blocks, SUBS, rows, virtuals), jnp.float32),
            pltpu.VMEM((blocks, SUBS, rows, virtuals), jnp.float32),
            pltpu.VMEM((slots, blocks, virtuals, virtuals), jnp.bfloat16),
            pltpu.VMEM((slots, virtuals, virtuals), jnp.float32),
            pltpu.VMEM((slots, 3, 3, half, wide), jnp.float32),
            pltpu.VMEM((slots, SIDE + 1, half, wide), jnp.float32),
            pltpu.VMEM((slots, SIDE + 1, half, wide), jnp.float32),
            dma((6, HOPS)),
            dma((6, HOPS)),
            dma,
            dma,
            dma,
            dma((2,)),
            dma((2,)),
            dma((slots, 3, 3)),
            dma((slots, 3, 3)),
            dma((slots, SIDE + 1)),
            dma((slots, SIDE + 1)),
            dma((slots, SIDE + 1)),
            dma((slots, SIDE + 1)),
            pltpu.VMEM((slots, half, virtuals), jnp.float32),
            pltpu.VMEM((devices, slots, thin, slim), jnp.float32),
            pltpu.VMEM((row_groups, slots, col_groups, thin, slim), jnp.float32),
            pltpu.VMEM((row_groups, slots, col_groups, thin, slim), jnp.float32),
            dma,
            dma,
            dma,
            dma,
        ],
        compiler_params=pltpu.CompilerParams(
            collective_id=0, has_side_effects=True, vmem_limit_bytes=58 << 20
        ),
    )(amplitudes.reshape(blocks, SUBS, rows, virtuals), integrals, tile_mask, pair_list)[1]


def body(amplitudes, integrals, tile_mask, pair_list):
    return residual_rows(amplitudes[0], integrals[0], tile_mask[0], pair_list.T)[None]


def solution(mesh):
    placed = (
        P("ia", "ka", None, None),
        P("ia", None, "ka", None, None),
        P("ia", None, "ka", None, None),
        P(),
    )
    return jax.shard_map(
        body, mesh=mesh, in_specs=placed, out_specs=P("ia", None, "ka", None), check_vma=False
    )
```

```python
import jax
import jax.numpy as jnp
from jax import lax
from jax.experimental import pallas as pl
from jax.experimental.pallas import tpu as pltpu
from jax.sharding import PartitionSpec as P

MESH = pl.DeviceIdType.MESH
HBM = pl.BlockSpec(memory_space=pl.ANY)

SIDE = 4
STEPS = ((1, 0, 0), (-1, 0, 0), (0, 1, 0), (0, -1, 0), (0, 0, 1), (0, 0, -1))
HOPS = 32
LAG = 2
MASK_FROM = 4
LATE = HOPS // 2
SUBS = 2 * HOPS
CROSS_OWN = 3
BAND = 256


def position():
    ia, ka = lax.axis_index("ia"), lax.axis_index("ka")
    return (ka % 2) * 2 + (ia // 2) % 2, ka // 2, ia // 4, ia % 2


def towards(x, y, z, way):
    dx, dy, dz = STEPS[way]
    return (x + dx + SIDE) % SIDE, (y + dy + SIDE) % SIDE, (z + dz + SIDE) % SIDE


def device(x, y, z, core):
    return z * 4 + (x % 2) * 2 + core, y * 2 + x // 2


def pick(test, then, other):
    return jnp.where(test, then, other)


def own_slot(index):
    return pick(index < CROSS_OWN, index, 2 * index - 2)


def relay_slot(index):
    return pick(index > HOPS // 2 - 3, index + HOPS // 2, 2 * index + 3)


def yz_rest(y, z, half, index):
    apart = (z - y + SIDE) % SIDE
    even = index % 2 == 0
    two_way = pick(half == 0, pick(even, 4, 5), pick(even, 2, 3))
    way = pick(apart == 1, pick(half == 0, 4, 3), pick(apart == 3, pick(half == 0, 5, 2), two_way))
    return way, pick(apart == 2, relay_slot(index // 2), index)


def x_rest(x, half, index):
    return pick(half == 0, 2 - x, x - 1), (index + LATE) % HOPS


def landing(x, y, z, half, index):
    inner = (x == 1) | (x == 2)
    by_x = inner & ((index < LATE) | (y == z))
    way, slot = yz_rest(y, z, half, index)
    x_way, x_slot = x_rest(x, half, index)
    return pick(by_x, x_way, way), pick(by_x, x_slot, slot)


def exchange(t_ref, land, m_buf, arrive, leave, m_sem, swap_arrive, swap_leave, work):
    x, y, z, core = position()
    inner = (x == 1) | (x == 2)
    apart = (z - y + SIDE) % SIDE
    alone = (apart == 0) & jnp.logical_not(inner)

    def swap(half):
        return pltpu.make_async_remote_copy(
            src_ref=t_ref.at[1 - core, pl.ds(half * HOPS, HOPS)],
            dst_ref=m_buf.at[core, pl.ds(half * HOPS, HOPS)],
            send_sem=swap_leave.at[half],
            recv_sem=swap_arrive.at[half],
            device_id=device(x, y, z, 1 - core),
            device_id_type=MESH,
        )

    @pl.when(alone)
    def _():
        swap(0).start()
        swap(1).start()
        pltpu.make_async_copy(t_ref.at[core], m_buf.at[core], m_sem).start()

    def landed(way, slot):
        pltpu.make_async_copy(land.at[way, slot], land.at[way, slot], arrive.at[way, slot]).wait()

    def send_own(way, slot, sub):
        for block in range(2):
            pltpu.make_async_remote_copy(
                src_ref=t_ref.at[block, sub],
                dst_ref=land.at[way, slot, core],
                send_sem=leave.at[way, slot],
                recv_sem=arrive.at[way, slot],
                device_id=device(*towards(x, y, z, way), block),
                device_id_type=MESH,
            ).start()

    def send_on(way, slot, from_way, from_slot):
        pltpu.make_async_remote_copy(
            src_ref=land.at[from_way, from_slot],
            dst_ref=land.at[way, slot],
            send_sem=leave.at[way, slot],
            recv_sem=arrive.at[way, slot],
            device_id=device(*towards(x, y, z, way), core),
            device_id_type=MESH,
        ).start()

    relay_from = {2: (5, -1, 4, 4), 3: (4, 5, 5, -1), 4: (3, 2, 2, -1), 5: (2, -1, 3, 3)}

    def by_apart(values):
        zero, one, two, three = values
        return pick(apart == 0, zero, pick(apart == 1, one, pick(apart == 2, two, three)))

    def yz_lag(way):
        return by_apart([0 if source < 0 or place == 2 else LAG for place, source in enumerate(relay_from[way])])

    lags = [
        pick(inner, 0, pick(x == 3, LAG, 2 * LAG)),
        pick(inner, 0, pick(x == 0, LAG, 2 * LAG)),
    ] + [yz_lag(way) for way in range(2, 6)]

    def step(t, carry):
        for way in range(6):
            slot = t - lags[way]
            active = (slot >= 0) & (slot < HOPS)
            if way < 2:
                half = pick(x == 1 + way, 0, 1)
                index = (slot + LATE) % HOPS
                from_t = inner & ((slot < LATE) | (apart == 0))
                sub = half * HOPS + index
                rest_way, rest_slot = yz_rest(y, z, half, index)
                from_way, from_slot = pick(inner, rest_way, way), pick(inner, rest_slot, slot)
            else:
                half = 0 if way < 4 else 1
                odd = way % 2
                early, late = slot < CROSS_OWN, slot > HOPS - 3
                relayed = late | (jnp.logical_not(early) & (slot % 2 == 1))
                own_index = pick(early, slot, (slot + 2) // 2)
                relay_index = pick(late, slot - HOPS // 2, (slot - 3) // 2)
                index = pick(apart == 2, 2 * own_index + odd, slot)
                places = relay_from[way]
                near_own = by_apart([places[0] < 0, places[1] < 0, False, places[3] < 0])
                own = pick(apart == 2, jnp.logical_not(relayed), near_own)
                from_t = own & (jnp.logical_not(inner) | (index < LATE))
                sub = half * HOPS + index
                x_way, x_slot = x_rest(x, half, index)
                relay_way = by_apart([max(place, 0) for place in places])
                from_way = pick(own, x_way, relay_way)
                from_slot = pick(own, x_slot, pick(apart == 2, own_slot(relay_index), slot))

            @pl.when(active & from_t)
            def _(way=way, slot=slot, sub=sub):
                send_own(way, slot, sub)

            @pl.when(active & jnp.logical_not(from_t))
            def _(way=way, slot=slot, from_way=from_way, from_slot=from_slot):
                landed(from_way, from_slot)
                send_on(way, slot, from_way, from_slot)

        work(t)
        return carry

    lax.fori_loop(0, HOPS + 2 * LAG, step, 0)

    @pl.when(jnp.logical_not(alone))
    def _():
        def finish(index, carry):
            for half in range(2):
                way, slot = landing(x, y, z, half, index)
                landed(way, slot)
                pltpu.make_async_copy(land.at[way, slot], m_buf.at[:, half * HOPS + index], m_sem).start()
            return carry

        lax.fori_loop(0, HOPS, finish, 0)
        pltpu.make_async_copy(m_buf, m_buf, m_sem).wait()

    @pl.when(alone)
    def _():
        swap(0).wait()
        swap(1).wait()
        pltpu.make_async_copy(t_ref.at[core], m_buf.at[core], m_sem).wait()


def drain_exchange(land, leave):
    def drain(slot, carry):
        for way in range(6):
            pltpu.make_async_copy(land.at[way, slot], land.at[way, slot], leave.at[way, slot]).wait()
        return carry

    lax.fori_loop(0, HOPS, drain, 0)


def cycle_kernel(
    t_ref, w_ref, mask_ref, pair_ref, land, out_ref,
    t_buf, m_buf, w_buf, o_buf, ring, relay, inbox,
    arrive, leave, t_sem, m_sem, w_sem, swap_arrive, swap_leave,
    ring_arrive, ring_leave, relay_arrive, relay_leave, inbox_arrive, inbox_leave,
    own, spread, stage, final, spread_arrive, spread_leave, final_arrive, final_leave,
):
    ring_sems, relay_sems, inbox_sems = (ring_arrive, ring_leave), (relay_arrive, relay_leave), (inbox_arrive, inbox_leave)
    x, y, z, core = position()
    slots, blocks, virtuals = w_buf.shape[0], w_buf.shape[1], w_buf.shape[2]

    row_groups, col_groups = lax.axis_size("ia"), lax.axis_size("ka")
    devices = row_groups * col_groups
    row, col = lax.axis_index("ia"), lax.axis_index("ka")
    barrier = pltpu.get_barrier_semaphore()

    def greet(n, carry):
        other = (row * col_groups + col + n) % devices
        pl.semaphore_signal(
            barrier, inc=1, device_id=(other // col_groups, other % col_groups), device_id_type=MESH
        )
        return carry

    lax.fori_loop(1, devices, greet, 0)
    pl.semaphore_wait(barrier, devices - 1)

    load_t = pltpu.make_async_copy(t_ref, t_buf, t_sem)
    load_w = pltpu.make_async_copy(w_ref, w_buf, w_sem)
    load_t.start()
    load_w.start()

    tiles = 8
    tile = virtuals // tiles

    def mask_band(n):
        s, block, r = n // (blocks * tiles), (n // tiles) % blocks, n % tiles
        band = pl.ds(pl.multiple_of(r * tile, tile), tile)
        for c in range(tiles):
            keep = mask_ref[s, block, r, c]
            columns = pl.ds(c * tile, tile)
            value = w_buf[s, block, band, columns]
            w_buf[s, block, band, columns] = jnp.where(keep != 0, value, jnp.zeros_like(value))

    def work(t):
        @pl.when(t == MASK_FROM)
        def _():
            load_t.wait()
            load_w.wait()

        @pl.when((t >= MASK_FROM) & (t < MASK_FROM + slots * blocks * tiles // 2))
        def _():
            mask_band(2 * (t - MASK_FROM))
            mask_band(2 * (t - MASK_FROM) + 1)

    exchange(t_ref, land, m_buf, arrive, leave, m_sem, swap_arrive, swap_leave, work)

    x_half = x // 2
    half = BAND // 2
    wide = virtuals // 2

    def band_of(s, k):
        return pick(s == 0, y + SIDE - 1 - k, y + 1 + k) % SIDE

    def block_of(s, k, chunk, side):
        offset = pick(chunk == 0, 1 - x_half, x_half) * half
        rows = pl.ds(pl.multiple_of(band_of(s, k) * BAND + offset, half), half)
        return o_buf.at[s, rows, pl.ds(side * wide, wide)]

    def y_beside(s):
        return device(x, (y + pick(s == 0, 1, SIDE - 1)) % SIDE, z, core)

    def x_beside(s):
        return device((x + pick(s == 0, 1, SIDE - 1)) % SIDE, y, z, core)

    def remote(source, target, sems, at, where):
        return pltpu.make_async_remote_copy(
            src_ref=source,
            dst_ref=target,
            send_sem=sems[1].at[at],
            recv_sem=sems[0].at[at],
            device_id=where,
            device_id_type=MESH,
        )

    def ring_copy(s, k, chunk):
        return remote(block_of(s, k, chunk, 0), ring.at[s, k, chunk], ring_sems, (s, k, chunk), y_beside(s))

    def last_relay(s):
        return remote(block_of(s, 3, 0, 0), relay.at[s, SIDE], relay_sems, (s, SIDE), x_beside(s))

    def relay_copy(s, k):
        return remote(block_of(s, k, 0, 1), relay.at[s, k], relay_sems, (s, k), x_beside(s))

    def pass_on(s, k):
        relay_copy(s, k).wait_recv()
        inbox_copy(s, k).start()

    def inbox_copy(s, k):
        return remote(relay.at[s, k], inbox.at[s, k], inbox_sems, (s, k), x_beside(s))

    def late_copy(s, k):
        return remote(block_of(s, k, 1, 1), ring.at[s, k, 2], ring_sems, (s, k, 2), y_beside(s))

    def add_left(s, k, chunk):
        ring_copy(s, k - 1, chunk).wait_recv()
        block = block_of(s, k, chunk, 0)
        block[...] = block[...] + ring[s, k - 1, chunk]

    def turn_left(s, k, chunk):
        add_left(s, k, chunk)
        ring_copy(s, k, chunk).start()

    def turn_right(s, k):
        inbox_copy(s, k).wait_recv()
        block = block_of(s, k, 1, 1)
        if k == 0:
            block[...] = block[...] + inbox[s, k]
        else:
            late_copy(s, k - 1).wait_recv()
            block[...] = block[...] + inbox[s, k] + ring[s, k - 1, 2]
        late_copy(s, k).start()

    def unit(u, carry):
        s = u % 2
        index = band_of(s, u // 2)
        band = pl.ds(pl.multiple_of(index * BAND, BAND), BAND)
        subs = BAND // t_buf.shape[2]
        total = jnp.zeros((2 * BAND, virtuals), jnp.float32)
        for block in range(blocks):
            mirrored = m_buf[block, :, :, band].reshape(virtuals, BAND).T
            mixed = 2.0 * t_buf[block, pl.ds(index * subs, subs)].reshape(BAND, virtuals) - mirrored
            high = mixed.astype(jnp.bfloat16)
            low = (mixed - high.astype(jnp.float32)).astype(jnp.bfloat16)
            pair = jnp.concatenate([high, low], axis=0)
            total += jnp.dot(pair, w_buf[s, block], preferred_element_type=jnp.float32)
        o_buf[s, band, :] = total[:BAND] + total[BAND:]
        relay_copy(s, u // 2).start()

        @pl.when(u < 2)
        def _():
            ring_copy(s, 0, 0).start()
            ring_copy(s, 0, 1).start()

        @pl.when((u == 2) | (u == 3))
        def _():
            pass_on(s, 0)

        @pl.when(u == 3)
        def _():
            turn_left(0, 1, 0)
            turn_left(1, 1, 0)

        @pl.when(u == 4)
        def _():
            turn_left(0, 1, 1)
            turn_left(1, 1, 1)

        @pl.when((u == 5) | (u == 6))
        def _():
            pass_on(1 - s, 1)
            turn_right(1 - s, 0)

        @pl.when(u == 6)
        def _():
            turn_left(0, 2, 0)
            turn_left(1, 2, 0)

        return carry

    lax.fori_loop(0, slots * SIDE, unit, 0)

    def both(step, *arguments):
        for s in range(2):
            step(s, *arguments)

    both(turn_left, 2, 1)
    both(pass_on, 2)
    both(turn_right, 1)
    for s in range(2):
        add_left(s, 3, 0)
        last_relay(s).start()
    both(pass_on, 3)
    both(turn_right, 2)
    both(add_left, 3, 1)
    for s in range(2):
        last_relay(s).wait_recv()
        inbox_copy(s, SIDE).start()
    thin, slim = half // row_groups, virtuals // col_groups

    def piece_of(to_row, to_col):
        rows = pl.ds(pl.multiple_of(to_row * thin, thin), thin)
        columns = pl.ds(pl.multiple_of(to_col * slim, slim), slim)
        return own.at[:, rows, columns]

    def scatter(side):
        span = col_groups // 2

        def send(n, carry):
            to_row = (row + n // span) % row_groups
            to_col = side * span + (col + n) % span
            target = spread.at[row * col_groups + col]

            @pl.when((to_row == row) & (to_col == col))
            def _():
                pltpu.make_async_copy(piece_of(to_row, to_col), target, spread_arrive).start()

            @pl.when((to_row != row) | (to_col != col))
            def _():
                pltpu.make_async_remote_copy(
                    src_ref=piece_of(to_row, to_col),
                    dst_ref=target,
                    send_sem=spread_leave,
                    recv_sem=spread_arrive,
                    device_id=(to_row, to_col),
                    device_id_type=MESH,
                ).start()

            return carry

        lax.fori_loop(0, row_groups * span, send, 0)

    for s in range(2):
        inbox_copy(s, 3).wait_recv()
        late_copy(s, 2).wait_recv()
        own[s, :, wide:] = block_of(s, 3, 1, 1)[...] + inbox[s, 3] + ring[s, 2, 2]
    scatter(1)
    for s in range(2):
        inbox_copy(s, SIDE).wait_recv()
        own[s, :, :wide] = block_of(s, 3, 1, 0)[...] + inbox[s, SIDE]
    scatter(0)
    pltpu.make_async_copy(spread, spread, spread_arrive).wait()

    def route(i, carry):
        for s in range(slots):
            j = pair_ref[s, i]
            t = jnp.where(pair_ref[0, j] == i, 0, 1)
            for k in range(col_groups):
                stage[i, s, k] = spread[j * col_groups + k, t]
        return carry

    lax.fori_loop(0, row_groups, route, 0)
    pltpu.make_async_copy(stage.at[row], final.at[row], final_arrive).start()

    def deliver(n, carry):
        to_row = (row + n) % row_groups
        pltpu.make_async_remote_copy(
            src_ref=stage.at[to_row],
            dst_ref=final.at[row],
            send_sem=final_leave,
            recv_sem=final_arrive,
            device_id=(to_row, col),
            device_id_type=MESH,
        ).start()
        return carry

    lax.fori_loop(1, row_groups, deliver, 0)

    for s in range(2):
        for k in range(3):
            ring_copy(s, k, 0).wait_send()
            ring_copy(s, k, 1).wait_send()
            late_copy(s, k).wait_send()
        for k in range(SIDE):
            relay_copy(s, k).wait_send()
            inbox_copy(s, k).wait_send()
        last_relay(s).wait_send()
        inbox_copy(s, SIDE).wait_send()
    drain_exchange(land, leave)
    sent = spread.at[pl.ds(0, devices - 1)]
    pltpu.make_async_copy(sent, sent, spread_leave).wait()

    pltpu.make_async_copy(final, final, final_arrive).wait()
    for s in range(slots):
        for k in range(col_groups):
            columns = pl.ds(k * half, half)
            out_ref[s, :, columns] = own[s, :, columns] + final[:, s, k].reshape(half, slim).T
    delivered = final.at[pl.ds(0, row_groups - 1)]
    pltpu.make_async_copy(delivered, delivered, final_leave).wait()


def residual_rows(amplitudes, integrals, tile_mask, pair_list):
    slots, blocks, virtuals = integrals.shape[0], integrals.shape[1], integrals.shape[2]
    rows = virtuals // SUBS
    half, wide = BAND // 2, virtuals // 2
    dma = pltpu.SemaphoreType.DMA
    row_groups, col_groups = lax.axis_size("ia"), lax.axis_size("ka")
    devices = row_groups * col_groups
    thin, slim = half // row_groups, virtuals // col_groups
    return pl.pallas_call(
        cycle_kernel,
        out_shape=(
            jax.ShapeDtypeStruct((6, HOPS, blocks, rows, virtuals), jnp.float32),
            pltpu.VMEM((slots, half, virtuals), jnp.float32),
        ),
        in_specs=[HBM, HBM, pl.BlockSpec(memory_space=pltpu.SMEM), pl.BlockSpec(memory_space=pltpu.SMEM)],
        out_specs=(HBM, pl.BlockSpec(memory_space=pltpu.VMEM)),
        scratch_shapes=[
            pltpu.VMEM((blocks, SUBS, rows, virtuals), jnp.float32),
            pltpu.VMEM((blocks, SUBS, rows, virtuals), jnp.float32),
            pltpu.VMEM((slots, blocks, virtuals, virtuals), jnp.bfloat16),
            pltpu.VMEM((slots, virtuals, virtuals), jnp.float32),
            pltpu.VMEM((slots, 3, 3, half, wide), jnp.float32),
            pltpu.VMEM((slots, SIDE + 1, half, wide), jnp.float32),
            pltpu.VMEM((slots, SIDE + 1, half, wide), jnp.float32),
            dma((6, HOPS)),
            dma((6, HOPS)),
            dma,
            dma,
            dma,
            dma((2,)),
            dma((2,)),
            dma((slots, 3, 3)),
            dma((slots, 3, 3)),
            dma((slots, SIDE + 1)),
            dma((slots, SIDE + 1)),
            dma((slots, SIDE + 1)),
            dma((slots, SIDE + 1)),
            pltpu.VMEM((slots, half, virtuals), jnp.float32),
            pltpu.VMEM((devices, slots, thin, slim), jnp.float32),
            pltpu.VMEM((row_groups, slots, col_groups, thin, slim), jnp.float32),
            pltpu.VMEM((row_groups, slots, col_groups, thin, slim), jnp.float32),
            dma,
            dma,
            dma,
            dma,
        ],
        compiler_params=pltpu.CompilerParams(
            collective_id=0, has_side_effects=True, vmem_limit_bytes=58 << 20
        ),
    )(amplitudes.reshape(blocks, SUBS, rows, virtuals), integrals, tile_mask, pair_list)[1]


def body(amplitudes, integrals, tile_mask, pair_list):
    return residual_rows(amplitudes[0], integrals[0], tile_mask[0], pair_list.T)[None]


def solution(mesh):
    placed = (
        P("ia", "ka", None, None),
        P("ia", None, "ka", None, None),
        P("ia", None, "ka", None, None),
        P(),
    )
    return jax.shard_map(
        body, mesh=mesh, in_specs=placed, out_specs=P("ia", None, "ka", None), check_vma=False
    )
```

```python
import jax
import jax.numpy as jnp
from jax import lax
from jax.experimental import pallas as pl
from jax.experimental.pallas import tpu as pltpu
from jax.sharding import PartitionSpec as P

MESH = pl.DeviceIdType.MESH
HBM = pl.BlockSpec(memory_space=pl.ANY)

SIDE = 4
STEPS = ((1, 0, 0), (-1, 0, 0), (0, 1, 0), (0, -1, 0), (0, 0, 1), (0, 0, -1))
HOPS = 32
LAG = 2
MASK_FROM = 4
LATE = HOPS // 2
SUBS = 2 * HOPS
CROSS_OWN = 3
BAND = 256


def position():
    ia, ka = lax.axis_index("ia"), lax.axis_index("ka")
    return (ka % 2) * 2 + (ia // 2) % 2, ka // 2, ia // 4, ia % 2


def towards(x, y, z, way):
    dx, dy, dz = STEPS[way]
    return (x + dx + SIDE) % SIDE, (y + dy + SIDE) % SIDE, (z + dz + SIDE) % SIDE


def device(x, y, z, core):
    return z * 4 + (x % 2) * 2 + core, y * 2 + x // 2


def pick(test, then, other):
    return jnp.where(test, then, other)


def own_slot(index):
    return pick(index < CROSS_OWN, index, 2 * index - 2)


def relay_slot(index):
    return pick(index > HOPS // 2 - 3, index + HOPS // 2, 2 * index + 3)


def yz_rest(y, z, half, index):
    apart = (z - y + SIDE) % SIDE
    even = index % 2 == 0
    two_way = pick(half == 0, pick(even, 4, 5), pick(even, 2, 3))
    way = pick(apart == 1, pick(half == 0, 4, 3), pick(apart == 3, pick(half == 0, 5, 2), two_way))
    return way, pick(apart == 2, relay_slot(index // 2), index)


def x_rest(x, half, index):
    return pick(half == 0, 2 - x, x - 1), (index + LATE) % HOPS


def landing(x, y, z, half, index):
    inner = (x == 1) | (x == 2)
    by_x = inner & ((index < LATE) | (y == z))
    way, slot = yz_rest(y, z, half, index)
    x_way, x_slot = x_rest(x, half, index)
    return pick(by_x, x_way, way), pick(by_x, x_slot, slot)


def exchange(t_ref, land, m_buf, arrive, leave, m_sem, swap_arrive, swap_leave, work):
    x, y, z, core = position()
    inner = (x == 1) | (x == 2)
    apart = (z - y + SIDE) % SIDE
    alone = (apart == 0) & jnp.logical_not(inner)

    def swap(half):
        return pltpu.make_async_remote_copy(
            src_ref=t_ref.at[1 - core, pl.ds(half * HOPS, HOPS)],
            dst_ref=m_buf.at[core, pl.ds(half * HOPS, HOPS)],
            send_sem=swap_leave.at[half],
            recv_sem=swap_arrive.at[half],
            device_id=device(x, y, z, 1 - core),
            device_id_type=MESH,
        )

    @pl.when(alone)
    def _():
        swap(0).start()
        swap(1).start()
        pltpu.make_async_copy(t_ref.at[core], m_buf.at[core], m_sem).start()

    def landed(way, slot):
        pltpu.make_async_copy(land.at[way, slot], land.at[way, slot], arrive.at[way, slot]).wait()

    def send_own(way, slot, sub):
        for block in range(2):
            pltpu.make_async_remote_copy(
                src_ref=t_ref.at[block, sub],
                dst_ref=land.at[way, slot, core],
                send_sem=leave.at[way, slot],
                recv_sem=arrive.at[way, slot],
                device_id=device(*towards(x, y, z, way), block),
                device_id_type=MESH,
            ).start()

    def send_on(way, slot, from_way, from_slot):
        pltpu.make_async_remote_copy(
            src_ref=land.at[from_way, from_slot],
            dst_ref=land.at[way, slot],
            send_sem=leave.at[way, slot],
            recv_sem=arrive.at[way, slot],
            device_id=device(*towards(x, y, z, way), core),
            device_id_type=MESH,
        ).start()

    relay_from = {2: (5, -1, 4, 4), 3: (4, 5, 5, -1), 4: (3, 2, 2, -1), 5: (2, -1, 3, 3)}

    def by_apart(values):
        zero, one, two, three = values
        return pick(apart == 0, zero, pick(apart == 1, one, pick(apart == 2, two, three)))

    def yz_lag(way):
        return by_apart([0 if source < 0 or place == 2 else LAG for place, source in enumerate(relay_from[way])])

    lags = [
        pick(inner, 0, pick(x == 3, LAG, 2 * LAG)),
        pick(inner, 0, pick(x == 0, LAG, 2 * LAG)),
    ] + [yz_lag(way) for way in range(2, 6)]

    def step(t, carry):
        for way in range(6):
            slot = t - lags[way]
            active = (slot >= 0) & (slot < HOPS)
            if way < 2:
                half = pick(x == 1 + way, 0, 1)
                index = (slot + LATE) % HOPS
                from_t = inner & ((slot < LATE) | (apart == 0))
                sub = half * HOPS + index
                rest_way, rest_slot = yz_rest(y, z, half, index)
                from_way, from_slot = pick(inner, rest_way, way), pick(inner, rest_slot, slot)
            else:
                half = 0 if way < 4 else 1
                odd = way % 2
                early, late = slot < CROSS_OWN, slot > HOPS - 3
                relayed = late | (jnp.logical_not(early) & (slot % 2 == 1))
                own_index = pick(early, slot, (slot + 2) // 2)
                relay_index = pick(late, slot - HOPS // 2, (slot - 3) // 2)
                index = pick(apart == 2, 2 * own_index + odd, slot)
                places = relay_from[way]
                near_own = by_apart([places[0] < 0, places[1] < 0, False, places[3] < 0])
                own = pick(apart == 2, jnp.logical_not(relayed), near_own)
                from_t = own & (jnp.logical_not(inner) | (index < LATE))
                sub = half * HOPS + index
                x_way, x_slot = x_rest(x, half, index)
                relay_way = by_apart([max(place, 0) for place in places])
                from_way = pick(own, x_way, relay_way)
                from_slot = pick(own, x_slot, pick(apart == 2, own_slot(relay_index), slot))

            @pl.when(active & from_t)
            def _(way=way, slot=slot, sub=sub):
                send_own(way, slot, sub)

            @pl.when(active & jnp.logical_not(from_t))
            def _(way=way, slot=slot, from_way=from_way, from_slot=from_slot):
                landed(from_way, from_slot)
                send_on(way, slot, from_way, from_slot)

        work(t)
        return carry

    lax.fori_loop(0, HOPS + 2 * LAG, step, 0)

    @pl.when(jnp.logical_not(alone))
    def _():
        def finish(index, carry):
            for half in range(2):
                way, slot = landing(x, y, z, half, index)
                landed(way, slot)
                pltpu.make_async_copy(land.at[way, slot], m_buf.at[:, half * HOPS + index], m_sem).start()
            return carry

        lax.fori_loop(0, HOPS, finish, 0)
        pltpu.make_async_copy(m_buf, m_buf, m_sem).wait()

    @pl.when(alone)
    def _():
        swap(0).wait()
        swap(1).wait()
        pltpu.make_async_copy(t_ref.at[core], m_buf.at[core], m_sem).wait()


def drain_exchange(land, leave):
    def drain(slot, carry):
        for way in range(6):
            pltpu.make_async_copy(land.at[way, slot], land.at[way, slot], leave.at[way, slot]).wait()
        return carry

    lax.fori_loop(0, HOPS, drain, 0)


def cycle_kernel(
    t_ref, w_ref, mask_ref, pair_ref, land, out_ref,
    t_buf, m_buf, w_buf, o_buf, ring, relay, inbox,
    arrive, leave, t_sem, m_sem, w_sem, swap_arrive, swap_leave,
    ring_arrive, ring_leave, relay_arrive, relay_leave, inbox_arrive, inbox_leave,
    own, spread, stage, final, spread_arrive, spread_leave, final_arrive, final_leave,
):
    ring_sems, relay_sems, inbox_sems = (ring_arrive, ring_leave), (relay_arrive, relay_leave), (inbox_arrive, inbox_leave)
    x, y, z, core = position()
    slots, blocks, virtuals = w_buf.shape[0], w_buf.shape[1], w_buf.shape[2]

    row_groups, col_groups = lax.axis_size("ia"), lax.axis_size("ka")
    devices = row_groups * col_groups
    row, col = lax.axis_index("ia"), lax.axis_index("ka")
    barrier = pltpu.get_barrier_semaphore()

    def greet(to_row, to_col):
        pl.semaphore_signal(barrier, inc=1, device_id=(to_row, to_col), device_id_type=MESH)

    def greet_row(n, carry):
        for to_col in range(col_groups):
            greet((row + n) % row_groups, to_col)
        return carry

    lax.fori_loop(1, row_groups, greet_row, 0)
    for turn in range(1, col_groups):
        greet(row, (col + turn) % col_groups)
    pl.semaphore_wait(barrier, devices - 1)

    load_t = pltpu.make_async_copy(t_ref, t_buf, t_sem)
    load_w = pltpu.make_async_copy(w_ref, w_buf, w_sem)
    load_t.start()
    load_w.start()

    tiles = 8
    tile = virtuals // tiles

    def mask_band(n):
        s, block, r = n // (blocks * tiles), (n // tiles) % blocks, n % tiles
        band = pl.ds(pl.multiple_of(r * tile, tile), tile)
        for c in range(tiles):
            keep = mask_ref[s, block, r, c]
            columns = pl.ds(c * tile, tile)
            value = w_buf[s, block, band, columns]
            w_buf[s, block, band, columns] = jnp.where(keep != 0, value, jnp.zeros_like(value))

    def work(t):
        @pl.when(t == MASK_FROM)
        def _():
            load_t.wait()
            load_w.wait()

        @pl.when((t >= MASK_FROM) & (t < MASK_FROM + slots * blocks * tiles // 2))
        def _():
            mask_band(2 * (t - MASK_FROM))
            mask_band(2 * (t - MASK_FROM) + 1)

    exchange(t_ref, land, m_buf, arrive, leave, m_sem, swap_arrive, swap_leave, work)

    x_half = x // 2
    half = BAND // 2
    wide = virtuals // 2

    def band_of(s, k):
        return pick(s == 0, y + SIDE - 1 - k, y + 1 + k) % SIDE

    def block_of(s, k, chunk, side):
        offset = pick(chunk == 0, 1 - x_half, x_half) * half
        rows = pl.ds(pl.multiple_of(band_of(s, k) * BAND + offset, half), half)
        return o_buf.at[s, rows, pl.ds(side * wide, wide)]

    def y_beside(s):
        return device(x, (y + pick(s == 0, 1, SIDE - 1)) % SIDE, z, core)

    def x_beside(s):
        return device((x + pick(s == 0, 1, SIDE - 1)) % SIDE, y, z, core)

    def remote(source, target, sems, at, where):
        return pltpu.make_async_remote_copy(
            src_ref=source,
            dst_ref=target,
            send_sem=sems[1].at[at],
            recv_sem=sems[0].at[at],
            device_id=where,
            device_id_type=MESH,
        )

    def ring_copy(s, k, chunk):
        return remote(block_of(s, k, chunk, 0), ring.at[s, k, chunk], ring_sems, (s, k, chunk), y_beside(s))

    def last_relay(s):
        return remote(block_of(s, 3, 0, 0), relay.at[s, SIDE], relay_sems, (s, SIDE), x_beside(s))

    def relay_copy(s, k):
        return remote(block_of(s, k, 0, 1), relay.at[s, k], relay_sems, (s, k), x_beside(s))

    def pass_on(s, k):
        relay_copy(s, k).wait_recv()
        inbox_copy(s, k).start()

    def inbox_copy(s, k):
        return remote(relay.at[s, k], inbox.at[s, k], inbox_sems, (s, k), x_beside(s))

    def late_copy(s, k):
        return remote(block_of(s, k, 1, 1), ring.at[s, k, 2], ring_sems, (s, k, 2), y_beside(s))

    def add_left(s, k, chunk):
        ring_copy(s, k - 1, chunk).wait_recv()
        block = block_of(s, k, chunk, 0)
        block[...] = block[...] + ring[s, k - 1, chunk]

    def turn_left(s, k, chunk):
        add_left(s, k, chunk)
        ring_copy(s, k, chunk).start()

    def turn_right(s, k):
        inbox_copy(s, k).wait_recv()
        block = block_of(s, k, 1, 1)
        if k == 0:
            block[...] = block[...] + inbox[s, k]
        else:
            late_copy(s, k - 1).wait_recv()
            block[...] = block[...] + inbox[s, k] + ring[s, k - 1, 2]
        late_copy(s, k).start()

    def unit(u, carry):
        s = u % 2
        index = band_of(s, u // 2)
        band = pl.ds(pl.multiple_of(index * BAND, BAND), BAND)
        subs = BAND // t_buf.shape[2]
        total = jnp.zeros((2 * BAND, virtuals), jnp.float32)
        for block in range(blocks):
            mirrored = m_buf[block, :, :, band].reshape(virtuals, BAND).T
            mixed = 2.0 * t_buf[block, pl.ds(index * subs, subs)].reshape(BAND, virtuals) - mirrored
            high = mixed.astype(jnp.bfloat16)
            low = (mixed - high.astype(jnp.float32)).astype(jnp.bfloat16)
            pair = jnp.concatenate([high, low], axis=0)
            total += jnp.dot(pair, w_buf[s, block], preferred_element_type=jnp.float32)
        o_buf[s, band, :] = total[:BAND] + total[BAND:]
        relay_copy(s, u // 2).start()

        @pl.when(u < 2)
        def _():
            ring_copy(s, 0, 0).start()
            ring_copy(s, 0, 1).start()

        @pl.when((u == 2) | (u == 3))
        def _():
            pass_on(s, 0)

        @pl.when(u == 3)
        def _():
            turn_left(0, 1, 0)
            turn_left(1, 1, 0)

        @pl.when(u == 4)
        def _():
            turn_left(0, 1, 1)
            turn_left(1, 1, 1)

        @pl.when((u == 5) | (u == 6))
        def _():
            pass_on(1 - s, 1)
            turn_right(1 - s, 0)

        @pl.when(u == 6)
        def _():
            turn_left(0, 2, 0)
            turn_left(1, 2, 0)

        return carry

    lax.fori_loop(0, slots * SIDE, unit, 0)

    def both(step, *arguments):
        for s in range(2):
            step(s, *arguments)

    both(turn_left, 2, 1)
    both(pass_on, 2)
    both(turn_right, 1)
    for s in range(2):
        add_left(s, 3, 0)
        last_relay(s).start()
    both(pass_on, 3)
    both(turn_right, 2)
    both(add_left, 3, 1)
    for s in range(2):
        last_relay(s).wait_recv()
        inbox_copy(s, SIDE).start()
    thin, slim = half // row_groups, virtuals // col_groups

    def piece_of(to_row, to_col):
        rows = pl.ds(pl.multiple_of(to_row * thin, thin), thin)
        columns = pl.ds(pl.multiple_of(to_col * slim, slim), slim)
        return own.at[:, rows, columns]

    def scatter(side):
        span = col_groups // 2

        def send(n, carry):
            to_row = (row + n // span) % row_groups
            to_col = side * span + (col + n) % span
            target = spread.at[row * col_groups + col]

            @pl.when((to_row == row) & (to_col == col))
            def _():
                pltpu.make_async_copy(piece_of(to_row, to_col), target, spread_arrive).start()

            @pl.when((to_row != row) | (to_col != col))
            def _():
                pltpu.make_async_remote_copy(
                    src_ref=piece_of(to_row, to_col),
                    dst_ref=target,
                    send_sem=spread_leave,
                    recv_sem=spread_arrive,
                    device_id=(to_row, to_col),
                    device_id_type=MESH,
                ).start()

            return carry

        lax.fori_loop(0, row_groups * span, send, 0)

    for s in range(2):
        inbox_copy(s, 3).wait_recv()
        late_copy(s, 2).wait_recv()
        own[s, :, wide:] = block_of(s, 3, 1, 1)[...] + inbox[s, 3] + ring[s, 2, 2]
    scatter(1)
    for s in range(2):
        inbox_copy(s, SIDE).wait_recv()
        own[s, :, :wide] = block_of(s, 3, 1, 0)[...] + inbox[s, SIDE]
    scatter(0)
    pltpu.make_async_copy(spread, spread, spread_arrive).wait()

    def route(i, carry):
        for s in range(slots):
            j = pair_ref[s, i]
            t = jnp.where(pair_ref[0, j] == i, 0, 1)
            for k in range(col_groups):
                stage[i, s, k] = spread[j * col_groups + k, t]
        return carry

    lax.fori_loop(0, row_groups, route, 0)
    pltpu.make_async_copy(stage.at[row], final.at[row], final_arrive).start()

    def deliver(n, carry):
        to_row = (row + n) % row_groups
        pltpu.make_async_remote_copy(
            src_ref=stage.at[to_row],
            dst_ref=final.at[row],
            send_sem=final_leave,
            recv_sem=final_arrive,
            device_id=(to_row, col),
            device_id_type=MESH,
        ).start()
        return carry

    lax.fori_loop(1, row_groups, deliver, 0)

    for s in range(2):
        for k in range(3):
            ring_copy(s, k, 0).wait_send()
            ring_copy(s, k, 1).wait_send()
            late_copy(s, k).wait_send()
        for k in range(SIDE):
            relay_copy(s, k).wait_send()
            inbox_copy(s, k).wait_send()
        last_relay(s).wait_send()
        inbox_copy(s, SIDE).wait_send()
    drain_exchange(land, leave)
    sent = spread.at[pl.ds(0, devices - 1)]
    pltpu.make_async_copy(sent, sent, spread_leave).wait()

    pltpu.make_async_copy(final, final, final_arrive).wait()
    for s in range(slots):
        for k in range(col_groups):
            columns = pl.ds(k * half, half)
            out_ref[s, :, columns] = own[s, :, columns] + final[:, s, k].reshape(half, slim).T
    delivered = final.at[pl.ds(0, row_groups - 1)]
    pltpu.make_async_copy(delivered, delivered, final_leave).wait()


def residual_rows(amplitudes, integrals, tile_mask, pair_list):
    slots, blocks, virtuals = integrals.shape[0], integrals.shape[1], integrals.shape[2]
    rows = virtuals // SUBS
    half, wide = BAND // 2, virtuals // 2
    dma = pltpu.SemaphoreType.DMA
    row_groups, col_groups = lax.axis_size("ia"), lax.axis_size("ka")
    devices = row_groups * col_groups
    thin, slim = half // row_groups, virtuals // col_groups
    return pl.pallas_call(
        cycle_kernel,
        out_shape=(
            jax.ShapeDtypeStruct((6, HOPS, blocks, rows, virtuals), jnp.float32),
            pltpu.VMEM((slots, half, virtuals), jnp.float32),
        ),
        in_specs=[HBM, HBM, pl.BlockSpec(memory_space=pltpu.SMEM), pl.BlockSpec(memory_space=pltpu.SMEM)],
        out_specs=(HBM, pl.BlockSpec(memory_space=pltpu.VMEM)),
        scratch_shapes=[
            pltpu.VMEM((blocks, SUBS, rows, virtuals), jnp.float32),
            pltpu.VMEM((blocks, SUBS, rows, virtuals), jnp.float32),
            pltpu.VMEM((slots, blocks, virtuals, virtuals), jnp.bfloat16),
            pltpu.VMEM((slots, virtuals, virtuals), jnp.float32),
            pltpu.VMEM((slots, 3, 3, half, wide), jnp.float32),
            pltpu.VMEM((slots, SIDE + 1, half, wide), jnp.float32),
            pltpu.VMEM((slots, SIDE + 1, half, wide), jnp.float32),
            dma((6, HOPS)),
            dma((6, HOPS)),
            dma,
            dma,
            dma,
            dma((2,)),
            dma((2,)),
            dma((slots, 3, 3)),
            dma((slots, 3, 3)),
            dma((slots, SIDE + 1)),
            dma((slots, SIDE + 1)),
            dma((slots, SIDE + 1)),
            dma((slots, SIDE + 1)),
            pltpu.VMEM((slots, half, virtuals), jnp.float32),
            pltpu.VMEM((devices, slots, thin, slim), jnp.float32),
            pltpu.VMEM((row_groups, slots, col_groups, thin, slim), jnp.float32),
            pltpu.VMEM((row_groups, slots, col_groups, thin, slim), jnp.float32),
            dma,
            dma,
            dma,
            dma,
        ],
        compiler_params=pltpu.CompilerParams(
            collective_id=0, has_side_effects=True, vmem_limit_bytes=58 << 20
        ),
    )(amplitudes.reshape(blocks, SUBS, rows, virtuals), integrals, tile_mask, pair_list)[1]


def body(amplitudes, integrals, tile_mask, pair_list):
    return residual_rows(amplitudes[0], integrals[0], tile_mask[0], pair_list.T)[None]


def solution(mesh):
    placed = (
        P("ia", "ka", None, None),
        P("ia", None, "ka", None, None),
        P("ia", None, "ka", None, None),
        P(),
    )
    return jax.shard_map(
        body, mesh=mesh, in_specs=placed, out_specs=P("ia", None, "ka", None), check_vma=False
    )
```
